256 devices in a mesh: ka: 8 (over x, core), gy: 8 (over z), gz: 4 (over y).
Axes of the slice: x: 4, y: 4, z: 8, core: 2. Of those that a mesh axis runs over, the one named last changes fastest.
Arguments:
- loads: float32 [128, 3, 256, 512], P('ka', None, 'gy', 'gz'), may hold values from -0.5 to 0.5
- sleeper_pos: int32 [128], P('ka'), may hold values from 0 to 127
- material: int32 [256, 512], P('gy', 'gz'), may hold values from 0 to 7, as said below
- material_table: float32 [8, 8], replicated, may hold values from -1 to 3, as said below
Outputs:
- adjoint_field: float32 [128, 2, 3, 256, 512], P('ka', None, None, 'gy', 'gz')
The draws below stay inside these ranges and needn't reach their ends.
Inputs may be any that keep to these rules, and one draw needn't show every extreme that they name: layered: the material index never falls with depth in a column, layer boundaries vary from column to column, and every material occurs. `material_table`: shifts and damping positive, each material's coupling matrix diagonally dominant with a positive diagonal.
All inputs are finite; a program needn't handle non-finite values.
Results may differ from the reference program's by a relative error of at most 0.0002.
Values sent between devices are 32-bit elements; how exact they have to be, the bound alone decides.
A program may use at most 128 MiB of HBM per device.

```python
import math
import jax
import jax.numpy as jnp
from jax import lax

KW = 128
NMAT = 8
SWEEPS = 2
DEG = 4
NY = 256
NZ = 512
SLEEPERS = 128


def draw_material(key, part):
    jitter = NZ // (4 * NMAT)
    offsets = jax.random.randint(key, (NMAT - 1, NY), -jitter, jitter + 1)
    boundary = (jnp.arange(1, NMAT, dtype=jnp.int32) * (NZ // NMAT))[:, None] + offsets
    depths = jnp.arange(NZ, dtype=jnp.int32)
    return jnp.sum((depths[None, None, :] >= boundary[:, :, None]).astype(jnp.int32), axis=0)


def draw_material_table(key, part):
    subkeys = jax.random.split(key, 4)
    diagonal_part = jnp.exp(jax.random.uniform(subkeys[0], (NMAT, 3), jnp.float32, jnp.log(0.5), jnp.log(3.0)))
    shifts = jnp.exp(jax.random.uniform(subkeys[1], (NMAT,), jnp.float32, jnp.log(0.05), jnp.log(1.0)))
    smallest = jnp.min(diagonal_part, axis=1)
    off_diagonal = jax.random.uniform(subkeys[2], (NMAT, 3), jnp.float32, -0.2, 0.2) * smallest[:, None]
    damping = jax.random.uniform(subkeys[3], (NMAT,), jnp.float32, 0.05, 0.3)
    return jnp.concatenate([shifts[:, None], diagonal_part, off_diagonal, damping[:, None]], axis=1)


def touch_ends(values, own_key, low, high):
    spot = [jax.random.randint(jax.random.fold_in(own_key, axis), (), 0, length) for axis, length in enumerate(values.shape)]
    main_axis = values.shape.index(max(values.shape))
    next_to = spot[:main_axis] + [(spot[main_axis] + 1) % values.shape[main_axis]] + spot[main_axis + 1:]
    return values.at[tuple(spot)].set(low).at[tuple(next_to)].set(high)


def block_scale(own_key, extent, shards, least, largest):
    gain, own = 1.0, jax.random.fold_in(own_key, 6)
    for axis_at, shards_of in shards:
        draws = jnp.exp(jax.random.uniform(jax.random.fold_in(own, axis_at), (shards_of,), jnp.float32, least / len(shards), largest / len(shards)))
        gain = gain * jnp.repeat(draws, extent[axis_at] // shards_of).reshape([-1 if axis == axis_at else 1 for axis in range(len(extent))])
    return gain


def noise(rng, extent, scale, bound, pieces=(), held_as=jnp.bfloat16):
    values = jax.random.normal(rng, extent, jnp.float32) * scale
    if len(pieces) > 0:
        values = block_scale(rng, extent, pieces, -0.22, 0.18) * values
    return jnp.clip(values, min=-bound, max=bound).astype(held_as)


def setup_inputs(seed: int = 0) -> dict:
    seeds = jax.random.split(jax.random.key(seed), 5)
    loads = noise(seeds[0], (SLEEPERS, 3, NY, NZ), SLEEPERS ** -0.5, 0.5, ((0, 8), (2, 8), (3, 4)), jnp.float32)
    sleeper_pos = touch_ends(jax.random.randint(seeds[1], (SLEEPERS,), 0, KW), jax.random.fold_in(seeds[1], 1), 0, KW - 1).astype(jnp.int32)
    material = draw_material(jax.random.fold_in(seeds[4], 71), 0)
    material_table = draw_material_table(jax.random.fold_in(seeds[4], 71), 0)
    return {"loads": loads, "sleeper_pos": sleeper_pos, "material": material, "material_table": material_table}


def local_operator(padded, wavefield, coefficients, wave_square):
    neighbours = padded[..., 2:, 1:-1] + padded[..., :-2, 1:-1] + padded[..., 1:-1, 2:] + padded[..., 1:-1, :-2]
    components = [wavefield[..., row_no, :, :] for row_no in range(3)]
    coupling_index = ((1, 4, 5), (4, 2, 6), (5, 6, 3))
    coupled = jnp.stack([sum(coefficients[coupling_index[row_no][column_no]] * components[column_no] for column_no in range(3)) for row_no in range(3)], axis=-3)
    real_op = 4.0 * wavefield - neighbours + coefficients[0] * wavefield + wave_square * coupled
    damping = coefficients[7] * wave_square * wavefield
    rotated = jnp.stack([-damping[..., 1, :, :, :], damping[..., 0, :, :, :]], axis=-4)
    return real_op + rotated


def spectral_bounds(material_table, squares):
    shifts = material_table[:, 0]
    diagonal_part = material_table[:, 1:4]
    off_diagonal = jnp.abs(material_table[:, 4:7])
    row_sums = jnp.stack([off_diagonal[:, 0] + off_diagonal[:, 1], off_diagonal[:, 0] + off_diagonal[:, 2], off_diagonal[:, 1] + off_diagonal[:, 2]], axis=1)
    gersh_low = jnp.min(diagonal_part - row_sums, axis=1)
    gersh_high = jnp.max(diagonal_part + row_sums, axis=1)
    lowest = jnp.min(shifts[:, None] + gersh_low[:, None] * squares[None, :], axis=0)
    highest = 8.0 + jnp.max(shifts[:, None] + gersh_high[:, None] * squares[None, :], axis=0)
    return lowest, highest


def wave_squares(waves):
    return (2.0 * jnp.sin(waves.astype(jnp.float32) * (math.pi / KW))) ** 2


def phase_table(positions, waves):
    turn_index = (positions[:, None] * waves[None, :]) % KW
    angles = turn_index.astype(jnp.float32) * (2.0 * math.pi / KW)
    return jnp.cos(angles), jnp.sin(angles)


def chebyshev(source, operate, lowest, highest):
    center = 0.5 * (highest + lowest)
    half_width = 0.5 * (highest - lowest)
    center_ratio = center / half_width
    solution = jnp.zeros_like(source)
    for sweep_no in range(SWEEPS):
        residual = source if sweep_no == 0 else source - operate(solution)
        weight = 1.0 / center_ratio
        direction = residual / center
        for inner_no in range(DEG):
            solution = solution + direction
            if inner_no + 1 < DEG:
                residual = residual - operate(direction)
                weight_next = 1.0 / (2.0 * center_ratio - weight)
                direction = (weight_next * weight) * direction + (2.0 * weight_next / half_width) * residual
                weight = weight_next
    return solution


def reference(loads, sleeper_pos, material, material_table):
    coefficients = jnp.moveaxis(material_table[material], -1, 0)
    waves = jnp.arange(KW, dtype=jnp.int32)
    cosines, sines = phase_table(sleeper_pos, waves)
    squares = wave_squares(waves)
    lowest, highest = spectral_bounds(material_table, squares)

    def solve_wave(inputs):
        cos_column, sin_column, wave_square, low_bound, high_bound = inputs
        real_part = jnp.tensordot(cos_column, loads, axes=(0, 0), precision=lax.Precision.HIGHEST)
        imag_part = -jnp.tensordot(sin_column, loads, axes=(0, 0), precision=lax.Precision.HIGHEST)
        source = jnp.stack([real_part, imag_part], axis=0)

        def operate(wavefield):
            padded = jnp.pad(wavefield, ((0, 0), (0, 0), (1, 1), (1, 1)))
            return local_operator(padded, wavefield, coefficients, wave_square)

        return chebyshev(source, operate, low_bound, high_bound)

    return lax.map(solve_wave, (cosines.T, sines.T, squares, lowest, highest))
```

```python
import math

import jax
import jax.numpy as jnp
from jax import lax
from jax.experimental import pallas as pl
from jax.experimental.pallas import tpu as pltpu
from jax.sharding import PartitionSpec as P

KW = 128
NMAT = 8
KA, GY, GZ = 8, 8, 4
LANES = 128
ROWS = 32
PART = ROWS // KA
STEPS = 7
MESH = pl.DeviceIdType.MESH
f32 = jnp.float32

LEAD = 3
ORDER = [(0, e) for e in range(LEAD)]
for e in range(STEPS):
    ORDER.append((1, e))
    if e + LEAD < STEPS:
        ORDER.append((0, e + LEAD))


def sine(angle):
    square = angle * angle
    value = jnp.full_like(angle, 1.0 / math.factorial(13))
    for degree in (11, 9, 7, 5, 3, 1):
        sign = -1.0 if (degree // 2) % 2 else 1.0
        value = value * square + sign / math.factorial(degree)
    return value * angle


def kernel(
    loads, pos, material, table, out,
    s1, r1, s2, wm, field, edge_out, edge_in, cells, coupling, per_k,
    p1_send, p1_recv, p2_send, p2_recv, halo_send, halo_recv,
):
    ka, gy, gz = lax.axis_index("ka"), lax.axis_index("gy"), lax.axis_index("gz")
    shape = (8, LANES)
    sub = lax.broadcasted_iota(jnp.int32, shape, 0)
    lane = lax.broadcasted_iota(jnp.int32, shape, 1)

    barrier = pltpu.get_barrier_semaphore()
    for o in range(1, KA):
        pl.semaphore_signal(
            barrier, inc=1, device_id={"ka": (ka + o) % KA}, device_id_type=MESH
        )
    for axis, at, size in (("gy", gy, GY), ("gz", gz, GZ)):
        for o in (1, size - 1):
            pl.semaphore_signal(
                barrier, inc=1, device_id={axis: (at + o) % size}, device_id_type=MESH
            )

    halves = []
    for h in range(2):
        position = jnp.zeros(shape, jnp.int32)
        for s in range(8):
            position = jnp.where(sub == s, pos[h * 8 + s], position)
        halves.append(position.astype(f32))

    def stage(o, carry):
        first = ((ka + o) % KA) * PART
        for h in range(2):
            s1[o, 0, h * 8 : h * 8 + 8, :] = halves[h]
            for yy in range(PART):
                for comp in range(3):
                    start = h * 8 * 96 + comp * ROWS + first + yy
                    s1[o, 1 + yy * 3 + comp, h * 8 : h * 8 + 8, :] = loads[
                        pl.ds(start, 8, stride=96), :
                    ]
        return carry

    lax.fori_loop(0, KA, stage, 0)
    zero = jnp.zeros(shape, f32)

    def clear_rows(row):
        for e in range(STEPS):
            for g in range(2):
                for c in range(6):
                    field[e, g, row, c] = zero

    def clear_columns(side):
        for e in range(STEPS):
            for g in range(2):
                for c in range(3):
                    edge_in[e, g, side, c] = zero

    pl.when(gy == 0)(lambda: clear_rows(0))
    pl.when(gy == GY - 1)(lambda: clear_rows(ROWS + 1))
    pl.when(gz == 0)(lambda: clear_columns(0))
    pl.when(gz == GZ - 1)(lambda: clear_columns(1))

    pl.semaphore_wait(barrier, KA - 1 + 4)

    def copy1(o):
        return pltpu.make_async_remote_copy(
            src_ref=s1.at[o],
            dst_ref=r1.at[ka],
            send_sem=p1_send.at[o],
            recv_sem=p1_recv.at[o],
            device_id={"ka": (ka + o) % KA},
            device_id_type=MESH,
        )

    def arrival1(o):
        return pltpu.make_async_remote_copy(
            src_ref=s1.at[o],
            dst_ref=r1.at[(ka + KA - o) % KA],
            send_sem=p1_send.at[o],
            recv_sem=p1_recv.at[o],
            device_id={"ka": (ka + o) % KA},
            device_id_type=MESH,
        )

    for o in (4, 3, 5, 2, 6, 1, 7):
        copy1(o).start()
    r1[ka] = s1[0]

    def gather_cells(t, carry):
        rows = pl.ds(pl.multiple_of(t * 8, 8), 8)
        index = material[rows, :]
        for f in range(8):
            value = jnp.zeros(shape, f32)
            for m in range(NMAT):
                value = jnp.where(index == m, table[m, f], value)
            cells[f, rows, :] = value
        return carry

    lax.fori_loop(0, ROWS // 8, gather_cells, 0)

    squares, centers = [], []
    for g in range(2):
        k = ka * 16 + g * 8 + sub
        half_turn = jnp.minimum(k, KW - k).astype(f32) * (math.pi / KW)
        root = 2.0 * sine(half_turn)
        q = root * root
        low, high = None, None
        for m in range(NMAT):
            entry = [jnp.full(shape, table[m, f], f32) for f in range(7)]
            off = [jnp.abs(entry[f]) for f in (4, 5, 6)]
            sums = (off[0] + off[1], off[0] + off[2], off[1] + off[2])
            lo = [entry[1 + c] - sums[c] for c in range(3)]
            hi = [entry[1 + c] + sums[c] for c in range(3)]
            lo = entry[0] + jnp.minimum(jnp.minimum(lo[0], lo[1]), lo[2]) * q
            hi = entry[0] + jnp.maximum(jnp.maximum(hi[0], hi[1]), hi[2]) * q
            low = lo if low is None else jnp.minimum(low, lo)
            high = hi if high is None else jnp.maximum(high, hi)
        high = 8.0 + high
        center = 0.5 * (high + low)
        width = 0.5 * (high - low)
        ratio = center / width
        weight = 1.0 / ratio
        d = [1.0 / center]
        r = [jnp.ones(shape, f32)]
        u = list(d)
        for _ in range(3):
            r = r + [zero]
            lowered = [center * d[j] if j < len(d) else zero for j in range(len(r))]
            raised = [zero] + d
            r = [r[j] - lowered[j] + raised[j] for j in range(len(r))]
            new_weight = 1.0 / (2.0 * ratio - weight)
            d = [
                (new_weight * weight) * (d[j] if j < len(d) else zero)
                + (2.0 * new_weight / width) * r[j]
                for j in range(len(r))
            ]
            u = [(u[j] if j < len(u) else zero) + d[j] for j in range(len(d))]
            weight = new_weight
        for j in range(4):
            per_k[g, j] = u[j]
        squares.append(q)
        centers.append(center)

    def prepare_coupling(y, carry):
        row = [cells[f, pl.ds(y, 1), :] for f in range(8)]
        for g in range(2):
            q = squares[g]
            base = centers[g] - 4.0 - row[0]
            for c in range(3):
                coupling[g, y, c] = base - q * row[1 + c]
                coupling[g, y, 3 + c] = -(q * row[4 + c])
            coupling[g, y, 6] = q * row[7]
        return carry

    lax.fori_loop(0, ROWS, prepare_coupling, 0)

    for o in range(1, KA):
        arrival1(o).wait_recv()
    positions = jnp.concatenate([r1[i, 0] for i in range(KA)], axis=0).T
    positions = jnp.concatenate([positions, positions], axis=0).astype(jnp.int32)
    wide = (256, LANES)
    row_no = lax.broadcasted_iota(jnp.int32, wide, 0)
    k_of = (row_no // 16) * 8 + row_no % 8
    imaginary = (row_no // 8) % 2
    turn = (k_of * positions + 32 * imaginary) & (KW - 1)
    away = jnp.abs(turn - KW // 2) - KW // 4
    weights = sine(away.astype(f32) * (2.0 * math.pi / KW))
    w_hi = weights.astype(jnp.bfloat16)
    w_lo = (weights - w_hi.astype(f32)).astype(jnp.bfloat16)
    wm[0:256, 0:128] = w_hi
    wm[0:256, 128:256] = w_hi
    wm[256:512, 0:128] = w_lo
    wm[256:512, 128:256] = jnp.zeros((256, 128), jnp.bfloat16)

    def transform(yy, carry):
        for comp in range(3):
            row = 1 + yy * 3 + comp
            values = jnp.concatenate([r1[i, row] for i in range(KA)], axis=0)
            v_hi = values.astype(jnp.bfloat16)
            v_lo = (values - v_hi.astype(f32)).astype(jnp.bfloat16)
            product = jnp.dot(
                wm[...], jnp.concatenate([v_hi, v_lo], axis=0), preferred_element_type=f32
            )
            product = product[0:256] + product[256:512]
            for d in range(KA):
                for g in range(2):
                    for ri in range(2):
                        at = ((d * 2 + g) * 2 + ri) * 8
                        s2[g, d, yy, ri * 3 + comp] = product[at : at + 8]
        return carry

    lax.fori_loop(0, PART, transform, 0)

    def copy2(g, o):
        return pltpu.make_async_remote_copy(
            src_ref=s2.at[g, (ka + o) % KA],
            dst_ref=field.at[0, g, pl.ds(1 + PART * ka, PART)],
            send_sem=p2_send.at[g, o],
            recv_sem=p2_recv.at[g, o],
            device_id={"ka": (ka + o) % KA},
            device_id_type=MESH,
        )

    def arrival2(g, o):
        return pltpu.make_async_remote_copy(
            src_ref=s2.at[g, (ka + o) % KA],
            dst_ref=field.at[0, g, pl.ds(1 + PART * ((ka + KA - o) % KA), PART)],
            send_sem=p2_send.at[g, o],
            recv_sem=p2_recv.at[g, o],
            device_id={"ka": (ka + o) % KA},
            device_id_type=MESH,
        )

    far_first = (4, 3, 5, 2, 6, 1, 7)
    for o in far_first:
        copy2(0, o).start()
    for g in range(2):
        field[0, g, pl.ds(1 + PART * ka, PART)] = s2[g, ka]
    for o in far_first:
        copy2(0, o).wait_send()
    for o in far_first:
        copy2(1, o).start()

    def row_copy(e, g, side):
        step = GY - 1 if side == 0 else 1
        return pltpu.make_async_remote_copy(
            src_ref=field.at[e, g, 1 if side == 0 else ROWS],
            dst_ref=field.at[e, g, ROWS + 1 if side == 0 else 0],
            send_sem=halo_send.at[e, g, side],
            recv_sem=halo_recv.at[e, g, side],
            device_id={"gy": (gy + step) % GY},
            device_id_type=MESH,
        )

    def row_arrival(e, g, side):
        step = GY - 1 if side == 0 else 1
        return pltpu.make_async_remote_copy(
            src_ref=field.at[e, g, 1 if side == 0 else ROWS],
            dst_ref=field.at[e, g, ROWS + 1 if side == 0 else 0],
            send_sem=halo_send.at[e, g, side],
            recv_sem=halo_recv.at[e, g, side],
            device_id={"gy": (gy + step) % GY},
            device_id_type=MESH,
        )

    def column_copy(e, g, side):
        step = GZ - 1 if side == 0 else 1
        return pltpu.make_async_remote_copy(
            src_ref=edge_out.at[e, g],
            dst_ref=edge_in.at[e, g, 1 - side],
            send_sem=halo_send.at[e, g, 2 + side],
            recv_sem=halo_recv.at[e, g, 2 + side],
            device_id={"gz": (gz + step) % GZ},
            device_id_type=MESH,
        )

    has_row = (gy > 0, gy < GY - 1)
    has_column = (gz > 0, gz < GZ - 1)

    def send_rows(e, g):
        for side in range(2):
            pl.when(has_row[side])(lambda: row_copy(e, g, side).start())

    def send_columns(e, g):
        for side in range(2):
            pl.when(has_column[side])(lambda: column_copy(e, g, side).start())

    def wait_halo(e, g):
        for side in range(2):
            pl.when(has_row[1 - side])(lambda: row_arrival(e, g, side).wait_recv())
            pl.when(has_column[1 - side])(lambda: column_copy(e, g, side).wait_recv())

    def finish(e, g):
        for side in range(2):
            pl.when(has_row[side])(lambda: row_copy(e, g, side).wait_send())
            pl.when(has_column[side])(lambda: column_copy(e, g, side).wait_send())

    owner = ((lane + 1) & (LANES - 1)) // 2
    even = (lane & 1) == 0
    first_lane = lane == 0
    last_lane = lane == LANES - 1

    def pack(packed, y, planes):
        real_at = owner == y
        imag_at = owner == y + ROWS
        return tuple(
            jnp.where(
                real_at,
                pltpu.roll(planes[c], 2 * y, 1),
                jnp.where(imag_at, pltpu.roll(planes[3 + c], 2 * y + 64, 1), packed[c]),
            )
            for c in range(3)
        )

    def receive(g):
        for o in far_first:
            arrival2(g, o).wait_recv()
        send_rows(0, g)

        def body(y, packed):
            return pack(packed, y, [field[0, g, y + 1, c] for c in range(6)])

        packed = lax.fori_loop(0, ROWS, body, (zero,) * 3, unroll=4)
        for c in range(3):
            edge_out[0, g, c] = packed[c]
        send_columns(0, g)

    def step(e, g):
        wait_halo(e, g)
        halo = []
        for c in range(3):
            halo.append(
                jnp.where(
                    even,
                    pltpu.roll(edge_in[e, g, 0, c], 1, 1),
                    pltpu.roll(edge_in[e, g, 1, c], LANES - 1, 1),
                )
            )
        scale = per_k[g, (2, 1, 0, 0, 2, 1, 0)[e]]
        outer = per_k[g, 3]

        def body(i, packed):
            y = (i * (ROWS - 1)) % ROWS
            here = [field[e, g, y + 1, c] for c in range(6)]
            k = [coupling[g, y, f] for f in range(7)]
            new = []
            for c in range(6):
                comp, other = c % 3, (c + 3) % 6
                side = pltpu.roll(
                    halo[comp], (2 * LANES - 2 * y) if c < 3 else (2 * LANES - 64 - 2 * y), 1
                )
                value = field[e, g, y, c] + field[e, g, y + 2, c]
                value += jnp.where(first_lane, side, pltpu.roll(here[c], 1, 1))
                value += jnp.where(last_lane, side, pltpu.roll(here[c], LANES - 1, 1))
                value += k[comp] * here[c]
                for j in range(3):
                    if j != comp:
                        value += k[2 + comp + j] * here[c - comp + j]
                if c < 3:
                    value += k[6] * here[other]
                else:
                    value -= k[6] * here[other]
                if e in (0, 4):
                    value = outer * value + scale * here[c]
                elif e in (1, 2):
                    value += scale * field[0, g, y + 1, c]
                elif e == 3:
                    value = field[0, g, y + 1, c] + (value - center_of(g) * here[c])
                else:
                    value += scale * field[4, g, y + 1, c]
                if e == 6:
                    value += field[3, g, y + 1, c]
                    out[pl.ds(g * 8 * 192 + c * ROWS + y, 8, stride=192), :] = value
                else:
                    field[e + 1, g, y + 1, c] = value
                new.append(value)
            return packed if e == 6 else pack(packed, y, new)

        if e == 6:
            lax.fori_loop(0, ROWS, body, (), unroll=2)
            return
        packed = lax.fori_loop(0, 2, body, (zero,) * 3)
        send_rows(e + 1, g)
        packed = lax.fori_loop(2, ROWS, body, packed, unroll=2)
        for c in range(3):
            edge_out[e + 1, g, c] = packed[c]
        send_columns(e + 1, g)

    def center_of(g):
        return centers[g]

    for g, e in ORDER:
        if e == 0:
            receive(g)
        step(e, g)

    for o in range(1, KA):
        copy1(o).wait_send()
        copy2(1, o).wait_send()
    for e in range(STEPS):
        for g in range(2):
            finish(e, g)


def local(loads, sleeper_pos, material, material_table):
    vmem = pl.BlockSpec(memory_space=pltpu.VMEM)
    smem = pl.BlockSpec(memory_space=pltpu.SMEM)
    dma = pltpu.SemaphoreType.DMA
    result = pl.pallas_call(
        kernel,
        out_shape=jax.ShapeDtypeStruct((16 * 6 * ROWS, LANES), f32),
        in_specs=[vmem, smem, vmem, smem],
        out_specs=vmem,
        scratch_shapes=[
            pltpu.VMEM((KA, 1 + 3 * PART, 16, LANES), f32),
            pltpu.VMEM((KA, 1 + 3 * PART, 16, LANES), f32),
            pltpu.VMEM((2, KA, PART, 6, 8, LANES), f32),
            pltpu.VMEM((512, 256), jnp.bfloat16),
            pltpu.VMEM((STEPS, 2, ROWS + 2, 6, 8, LANES), f32),
            pltpu.VMEM((STEPS, 2, 3, 8, LANES), f32),
            pltpu.VMEM((STEPS, 2, 2, 3, 8, LANES), f32),
            pltpu.VMEM((8, ROWS, LANES), f32),
            pltpu.VMEM((2, ROWS, 7, 8, LANES), f32),
            pltpu.VMEM((2, 4, 8, LANES), f32),
            dma((KA,)),
            dma((KA,)),
            dma((2, KA)),
            dma((2, KA)),
            dma((STEPS, 2, 4)),
            dma((STEPS, 2, 4)),
        ],
        compiler_params=pltpu.CompilerParams(
            collective_id=0, has_side_effects=True, vmem_limit_bytes=40 * 2**20
        ),
        name="adjoint",
    )(loads.reshape(16 * 3 * ROWS, LANES), sleeper_pos, material, material_table)
    return result.reshape(16, 2, 3, ROWS, LANES)


def solution(mesh):
    return jax.shard_map(
        local,
        mesh=mesh,
        in_specs=(P("ka", None, "gy", "gz"), P("ka"), P("gy", "gz"), P()),
        out_specs=P("ka", None, None, "gy", "gz"),
        check_vma=False,
    )
```

```python
import math

import jax
import jax.numpy as jnp
from jax import lax
from jax.experimental import pallas as pl
from jax.experimental.pallas import tpu as pltpu
from jax.sharding import PartitionSpec as P

KW = 128
NMAT = 8
KA, GY, GZ = 8, 8, 4
LANES = 128
ROWS = 32
PART = ROWS // KA
STEPS = 7
STRIP = 21
TOP, LEFT, RIGHT, ALL_ROWS = 8, 49, 59, 68
MESH = pl.DeviceIdType.MESH
f32 = jnp.float32


def sine(angle):
    square = angle * angle
    value = jnp.full_like(angle, 1.0 / math.factorial(13))
    for degree in (11, 9, 7, 5, 3, 1):
        sign = -1.0 if (degree // 2) % 2 else 1.0
        value = value * square + sign / math.factorial(degree)
    return value * angle


def kernel(
    loads, pos, material, table, out,
    s1, r1, s2, wm, f_b, f_a, f_c, f_u, f_r,
    strip_out, strip_in, corner_out, corner_in, mat, mat_in, mask, cells, coupling, per_k,
    p1_send, p1_recv, p2_send, p2_recv, halo_send, halo_recv, mat_send, mat_recv,
):
    ka, gy, gz = lax.axis_index("ka"), lax.axis_index("gy"), lax.axis_index("gz")
    shape = (8, LANES)
    sub = lax.broadcasted_iota(jnp.int32, shape, 0)
    lane = lax.broadcasted_iota(jnp.int32, shape, 1)

    barrier = pltpu.get_barrier_semaphore()
    for o in range(1, KA):
        pl.semaphore_signal(
            barrier, inc=1, device_id={"ka": (ka + o) % KA}, device_id_type=MESH
        )
    for dy in (-1, 0, 1):
        for dz in (-1, 0, 1):
            if dy or dz:
                pl.semaphore_signal(
                    barrier,
                    inc=1,
                    device_id={"gy": (gy + dy + GY) % GY, "gz": (gz + dz + GZ) % GZ},
                    device_id_type=MESH,
                )

    halves = []
    for h in range(2):
        position = jnp.zeros(shape, jnp.int32)
        for s in range(8):
            position = jnp.where(sub == s, pos[h * 8 + s], position)
        halves.append(position.astype(f32))

    def stage(o, carry):
        first = ((ka + o) % KA) * PART
        for h in range(2):
            s1[o, 0, h * 8 : h * 8 + 8, :] = halves[h]
            for yy in range(PART):
                for comp in range(3):
                    start = h * 8 * 96 + comp * ROWS + first + yy
                    s1[o, 1 + yy * 3 + comp, h * 8 : h * 8 + 8, :] = loads[
                        pl.ds(start, 8, stride=96), :
                    ]
        return carry

    lax.fori_loop(0, KA, stage, 0)
    zero = jnp.zeros(shape, f32)

    def clear_rows(first):
        def body(row, carry):
            for buffer in (f_b, f_a, f_c, f_u, f_r):
                for g in range(2):
                    for c in range(6):
                        buffer[g, row, c] = zero
            return carry

        lax.fori_loop(first, first + 8, body, 0)

    pl.when(gy == 0)(lambda: clear_rows(0))
    pl.when(gy == GY - 1)(lambda: clear_rows(TOP + ROWS))
    for t in range(ROWS // 8):
        mat[1 + t] = material[8 * t : 8 * t + 8, :]

    pl.semaphore_wait(barrier, KA - 1 + 8)

    exists = {-1: gy > 0, 1: gy < GY - 1}, {-1: gz > 0, 1: gz < GZ - 1}

    def send(src, dst, dy, dz, sends, recvs, at):
        copy = pltpu.make_async_remote_copy(
            src_ref=src,
            dst_ref=dst,
            send_sem=sends.at[at],
            recv_sem=recvs.at[at],
            device_id={"gy": (gy + dy + GY) % GY, "gz": (gz + dz + GZ) % GZ},
            device_id_type=MESH,
        )
        to, origin = True, True
        if dy:
            to, origin = exists[0][dy], exists[0][-dy]
        if dz:
            to = exists[1][dz] if to is True else jnp.logical_and(to, exists[1][dz])
            origin = exists[1][-dz] if origin is True else jnp.logical_and(origin, exists[1][-dz])
        return copy, to, origin

    def start(message):
        pl.when(message[1])(lambda: message[0].start())

    def finish(message):
        pl.when(message[1])(lambda: message[0].wait_send())

    def receive(message):
        pl.when(message[2])(lambda: message[0].wait_recv())

    mat_rows = (
        send(mat.at[1], mat.at[5], -1, 0, mat_send, mat_recv, 0),
        send(mat.at[4], mat.at[0], 1, 0, mat_send, mat_recv, 1),
    )
    mat_strips = (
        send(mat.at[6], mat_in.at[0], 0, 1, mat_send, mat_recv, 2),
        send(mat.at[7], mat_in.at[1], 0, -1, mat_send, mat_recv, 3),
    )
    for message in mat_rows:
        start(message)

    def copy1(o):
        return pltpu.make_async_remote_copy(
            src_ref=s1.at[o],
            dst_ref=r1.at[ka],
            send_sem=p1_send.at[o],
            recv_sem=p1_recv.at[o],
            device_id={"ka": (ka + o) % KA},
            device_id_type=MESH,
        )

    def arrival1(o):
        return pltpu.make_async_remote_copy(
            src_ref=s1.at[o],
            dst_ref=r1.at[(ka + KA - o) % KA],
            send_sem=p1_send.at[o],
            recv_sem=p1_recv.at[o],
            device_id={"ka": (ka + o) % KA},
            device_id_type=MESH,
        )

    for o in (4, 3, 5, 2, 6, 1, 7):
        copy1(o).start()
    r1[ka] = s1[0]

    block = lane // STRIP
    place = lane - block * STRIP
    for message in mat_rows:
        receive(message)
    for side in range(2):
        value = mat[5]
        value = pltpu.roll(value, (STRIP * 5 + 7 + 7 * side) % LANES, 1)
        for j in range(5):
            value = jnp.where(block == j, pltpu.roll(mat[j], STRIP * j + 7 + 7 * side, 1), value)
        mat[6 + side] = value
    for message in mat_strips:
        start(message)

    for side in range(2):
        row = gy * ROWS + 8 * block - 8
        column = gz * LANES + place + (LANES - 14 if side else -7)
        inside = jnp.logical_and(column >= 0, column < GZ * LANES)
        inside = jnp.logical_and(inside, block < 6)
        for i in range(8):
            valid = jnp.logical_and(row + i >= 0, row + i < GY * ROWS)
            if i == 0:
                valid = jnp.logical_and(valid, block > 0)
            if i == 7:
                valid = jnp.logical_and(valid, block < 5)
            mask[side, i] = jnp.where(jnp.logical_and(inside, valid), 1.0, 0.0)

    squares, centers = [], []
    for g in range(2):
        k = ka * 16 + g * 8 + sub
        half_turn = jnp.minimum(k, KW - k).astype(f32) * (math.pi / KW)
        root = 2.0 * sine(half_turn)
        q = root * root
        low, high = None, None
        for m in range(NMAT):
            entry = [jnp.full(shape, table[m, f], f32) for f in range(7)]
            off = [jnp.abs(entry[f]) for f in (4, 5, 6)]
            sums = (off[0] + off[1], off[0] + off[2], off[1] + off[2])
            lo = [entry[1 + c] - sums[c] for c in range(3)]
            hi = [entry[1 + c] + sums[c] for c in range(3)]
            lo = entry[0] + jnp.minimum(jnp.minimum(lo[0], lo[1]), lo[2]) * q
            hi = entry[0] + jnp.maximum(jnp.maximum(hi[0], hi[1]), hi[2]) * q
            low = lo if low is None else jnp.minimum(low, lo)
            high = hi if high is None else jnp.maximum(high, hi)
        high = 8.0 + high
        center = 0.5 * (high + low)
        width = 0.5 * (high - low)
        ratio = center / width
        weight = 1.0 / ratio
        d = [1.0 / center]
        r = [jnp.ones(shape, f32)]
        u = list(d)
        for _ in range(3):
            r = r + [zero]
            lowered = [center * d[j] if j < len(d) else zero for j in range(len(r))]
            raised = [zero] + d
            r = [r[j] - lowered[j] + raised[j] for j in range(len(r))]
            new_weight = 1.0 / (2.0 * ratio - weight)
            d = [
                (new_weight * weight) * (d[j] if j < len(d) else zero)
                + (2.0 * new_weight / width) * r[j]
                for j in range(len(r))
            ]
            u = [(u[j] if j < len(u) else zero) + d[j] for j in range(len(d))]
            weight = new_weight
        for j in range(4):
            per_k[g, j] = u[j]
        per_k[g, 4] = center
        squares.append(q)
        centers.append(center)

    for message in mat_strips:
        receive(message)
    foreign = (place < 7, place >= 14)
    mat_strip = [jnp.where(foreign[side], mat_in[side], mat[6 + side]) for side in range(2)]

    def gather_cells(t, carry):
        index = mat[t]
        rows = pl.ds(pl.multiple_of(t * 8, 8), 8)
        for f in range(8):
            value = jnp.zeros(shape, f32)
            for m in range(NMAT):
                value = jnp.where(index == m, table[m, f], value)
            cells[f, rows, :] = value
        return carry

    lax.fori_loop(0, 6, gather_cells, 0)
    for side in range(2):
        for f in range(8):
            value = jnp.zeros(shape, f32)
            for m in range(NMAT):
                value = jnp.where(mat_strip[side] == m, table[m, f], value)
            cells[f, 48 + 8 * side : 56 + 8 * side, :] = value

    def prepare_coupling(y, carry):
        row = [cells[f, pl.ds(y, 1), :] for f in range(8)]
        for g in range(2):
            q = squares[g]
            base = centers[g] - 4.0 - row[0]
            for c in range(3):
                coupling[g, y, c] = base - q * row[1 + c]
                coupling[g, y, 3 + c] = -(q * row[4 + c])
            coupling[g, y, 6] = q * row[7]
        return carry

    lax.fori_loop(0, 64, prepare_coupling, 0)

    for o in range(1, KA):
        arrival1(o).wait_recv()
    positions = jnp.concatenate([r1[i, 0] for i in range(KA)], axis=0).T
    positions = jnp.concatenate([positions, positions], axis=0).astype(jnp.int32)
    wide = (256, LANES)
    row_no = lax.broadcasted_iota(jnp.int32, wide, 0)
    k_of = (row_no // 16) * 8 + row_no % 8
    imaginary = (row_no // 8) % 2
    turn = (k_of * positions + 32 * imaginary) & (KW - 1)
    away = jnp.abs(turn - KW // 2) - KW // 4
    weights = sine(away.astype(f32) * (2.0 * math.pi / KW))
    w_hi = weights.astype(jnp.bfloat16)
    w_lo = (weights - w_hi.astype(f32)).astype(jnp.bfloat16)
    wm[0:256, 0:128] = w_hi
    wm[0:256, 128:256] = w_hi
    wm[256:512, 0:128] = w_lo
    wm[256:512, 128:256] = jnp.zeros((256, 128), jnp.bfloat16)

    def transform(yy, carry):
        for comp in range(3):
            row = 1 + yy * 3 + comp
            values = jnp.concatenate([r1[i, row] for i in range(KA)], axis=0)
            v_hi = values.astype(jnp.bfloat16)
            v_lo = (values - v_hi.astype(f32)).astype(jnp.bfloat16)
            product = jnp.dot(
                wm[...], jnp.concatenate([v_hi, v_lo], axis=0), preferred_element_type=f32
            )
            product = product[0:256] + product[256:512]
            for d in range(KA):
                for g in range(2):
                    for ri in range(2):
                        at = ((d * 2 + g) * 2 + ri) * 8
                        s2[g, d, yy, ri * 3 + comp] = product[at : at + 8]
        return carry

    lax.fori_loop(0, PART, transform, 0)

    def copy2(g, o):
        return pltpu.make_async_remote_copy(
            src_ref=s2.at[g, (ka + o) % KA],
            dst_ref=f_b.at[g, pl.ds(TOP + PART * ka, PART)],
            send_sem=p2_send.at[g, o],
            recv_sem=p2_recv.at[g, o],
            device_id={"ka": (ka + o) % KA},
            device_id_type=MESH,
        )

    def arrival2(g, o):
        return pltpu.make_async_remote_copy(
            src_ref=s2.at[g, (ka + o) % KA],
            dst_ref=f_b.at[g, pl.ds(TOP + PART * ((ka + KA - o) % KA), PART)],
            send_sem=p2_send.at[g, o],
            recv_sem=p2_recv.at[g, o],
            device_id={"ka": (ka + o) % KA},
            device_id_type=MESH,
        )

    far_first = (4, 3, 5, 2, 6, 1, 7)
    for o in far_first:
        copy2(0, o).start()
    for g in range(2):
        f_b[g, pl.ds(TOP + PART * ka, PART)] = s2[g, ka]
    for o in far_first:
        copy2(0, o).wait_send()
    for o in far_first:
        copy2(1, o).start()

    def messages(g):
        rows = (
            send(f_b.at[g, pl.ds(TOP, 7)], f_b.at[g, pl.ds(TOP + ROWS, 7)], -1, 0, halo_send, halo_recv, (g, 0)),
            send(f_b.at[g, pl.ds(TOP + ROWS - 7, 7)], f_b.at[g, pl.ds(1, 7)], 1, 0, halo_send, halo_recv, (g, 1)),
        )
        sides = (
            send(strip_out.at[g, 0], strip_in.at[g, 0], 0, 1, halo_send, halo_recv, (g, 2)),
            send(strip_out.at[g, 1], strip_in.at[g, 1], 0, -1, halo_send, halo_recv, (g, 3)),
        )
        corners = tuple(
            send(corner_out.at[g, n // 2], corner_in.at[g, n], dy, dz, halo_send, halo_recv, (g, 4 + n))
            for n, (dy, dz) in enumerate(((1, 1), (1, -1), (-1, 1), (-1, -1)))
        )
        return rows, sides + corners

    def exchange(g):
        for o in far_first:
            arrival2(g, o).wait_recv()
        rows, others = messages(g)
        for message in rows:
            start(message)

        def body(c, carry):
            near = [zero, zero]
            for i in range(8):
                values = [f_b[g, TOP + 8 * j + i, c] for j in range(4)]
                for side in range(2):
                    shift = 7 + 7 * side
                    strip = pltpu.roll(values[3], (STRIP * 4 + shift) % LANES, 1)
                    for j in (2, 1, 0):
                        strip = jnp.where(
                            block <= j + 1, pltpu.roll(values[j], STRIP * (j + 1) + shift, 1), strip
                        )
                    strip_out[g, side, i, c] = strip
                here = jnp.logical_and(lane >= 14 * i, lane < 14 * i + 14)
                near[0] = jnp.where(here, pltpu.roll(values[3], 14 * i + 7, 1), near[0])
                near[1] = jnp.where(here, pltpu.roll(values[0], 14 * i + 7, 1), near[1])
            corner_out[g, 0, c] = near[0]
            corner_out[g, 1, c] = near[1]
            return carry

        lax.fori_loop(0, 6, body, 0)
        for message in others:
            start(message)

    inner_block = jnp.logical_and(block >= 1, block <= 4)

    def wrap_strips(buffer, g, c):
        for first in (LEFT, RIGHT):
            buffer[g, first - 1, c] = pltpu.roll(buffer[g, first + 7, c], STRIP, 1)
            buffer[g, first + 8, c] = pltpu.roll(buffer[g, first, c], LANES - STRIP, 1)

    def assemble(g):
        masks = [[mask[side, i] > 0.5 for i in range(8)] for side in range(2)]

        def body(c, carry):
            for i in range(8):
                above, below = f_b[g, i, c], f_b[g, TOP + ROWS + i, c]
                for side in range(2):
                    shift = 7 + 7 * side
                    own = jnp.where(
                        block == 0,
                        pltpu.roll(above, shift, 1),
                        jnp.where(
                            block == 5,
                            pltpu.roll(below, (STRIP * 5 + shift) % LANES, 1),
                            strip_out[g, side, i, c],
                        ),
                    )
                    lower = 2 * LANES + 7 * side - 14 * i
                    other = jnp.where(
                        block == 0,
                        pltpu.roll(corner_in[g, side, c], lower % LANES, 1),
                        jnp.where(
                            block == 5,
                            pltpu.roll(corner_in[g, 2 + side, c], (lower + STRIP * 5) % LANES, 1),
                            strip_in[g, side, i, c],
                        ),
                    )
                    value = jnp.where(foreign[side], other, own)
                    f_b[g, (LEFT, RIGHT)[side] + i, c] = jnp.where(masks[side][i], value, 0.0)
            wrap_strips(f_b, g, c)
            return carry

        lax.fori_loop(0, 6, body, 0)

    source = (f_b, f_a, f_c, f_u, f_r, f_a, f_c)
    target = (f_a, f_c, f_u, f_r, f_a, f_c, f_a)

    def advance(e, g, at, cell, keep=None):
        src = source[e]
        here = [src[g, at, c] for c in range(6)]
        k = [coupling[g, cell, f] for f in range(7)]
        scale = per_k[g, (2, 1, 0, 4, 2, 1, 0)[e]]
        for c in range(6):
            comp, other = c % 3, (c + 3) % 6
            value = src[g, at - 1, c] + src[g, at + 1, c]
            value += pltpu.roll(here[c], 1, 1) + pltpu.roll(here[c], LANES - 1, 1)
            value += k[comp] * here[c]
            for j in range(3):
                if j != comp:
                    value += k[2 + comp + j] * here[c - comp + j]
            if c < 3:
                value += k[6] * here[other]
            else:
                value -= k[6] * here[other]
            if e in (0, 4):
                value = per_k[g, 3] * value + scale * here[c]
            elif e in (1, 2):
                value += scale * f_b[g, at, c]
            elif e == 3:
                value = f_b[g, at, c] + (value - scale * here[c])
            else:
                value += scale * f_r[g, at, c]
            if e == 6:
                value += f_u[g, at, c]
            if keep is not None:
                value *= keep
            target[e][g, at, c] = value

    def main_rows(e, g, first, count, unroll):
        def body(i, carry):
            advance(e, g, i + first, i + first)
            return carry

        lax.fori_loop(0, count, body, 0, unroll=unroll)

    def interior(g):
        for e in range(STEPS):
            main_rows(e, g, TOP + e + 1, 30 - 2 * e, (5, 4, 2, 4, 2, 5, 3)[e])

    def borders(g):
        for e in range(STEPS):
            beyond = 6 - e
            if beyond:
                pl.when(gy > 0)(lambda: main_rows(e, g, TOP - beyond, beyond, beyond))
                pl.when(gy < GY - 1)(lambda: main_rows(e, g, TOP + ROWS, beyond, beyond))
            main_rows(e, g, TOP, e + 1, e + 1)
            main_rows(e, g, TOP + ROWS - e - 1, e + 1, e + 1)

    def strips(g):
        for e in range(STEPS):

            def body(i, carry):
                advance(e, g, LEFT + i, 48 + i, mask[0, i])
                advance(e, g, RIGHT + i, 56 + i, mask[1, i])
                return carry

            lax.fori_loop(0, 8, body, 0, unroll=4)
            for c in range(6):
                wrap_strips(target[e], g, c)

    def deliver(g):
        edge = jnp.logical_or(lane < 7, lane >= LANES - 7)

        def body(i, carry):
            for c in range(6):
                joined = jnp.where(
                    place < 7, pltpu.roll(f_a[g, RIGHT + i, c], LANES - 7, 1), f_a[g, LEFT + i, c]
                )
                for j in range(4):
                    y = 8 * j + i
                    value = jnp.where(
                        edge,
                        pltpu.roll(joined, (2 * LANES - STRIP * (j + 1) - 7) % LANES, 1),
                        f_a[g, TOP + y, c],
                    )
                    out[pl.ds(g * 8 * 192 + c * ROWS + y, 8, stride=192), :] = value
            return carry

        lax.fori_loop(0, 8, body, 0)

    def await_halo(g):
        for group in messages(g):
            for message in group:
                receive(message)

    exchange(0)
    interior(0)
    await_halo(0)
    borders(0)
    exchange(1)
    assemble(0)
    strips(0)
    deliver(0)
    interior(1)
    await_halo(1)
    borders(1)
    assemble(1)
    strips(1)
    deliver(1)

    for o in range(1, KA):
        copy1(o).wait_send()
        copy2(1, o).wait_send()
    for message in mat_rows + mat_strips:
        finish(message)
    for g in range(2):
        for group in messages(g):
            for message in group:
                finish(message)


def local(loads, sleeper_pos, material, material_table):
    vmem = pl.BlockSpec(memory_space=pltpu.VMEM)
    smem = pl.BlockSpec(memory_space=pltpu.SMEM)
    dma = pltpu.SemaphoreType.DMA
    result = pl.pallas_call(
        kernel,
        out_shape=jax.ShapeDtypeStruct((16 * 6 * ROWS, LANES), f32),
        in_specs=[vmem, smem, vmem, smem],
        out_specs=vmem,
        scratch_shapes=[
            pltpu.VMEM((KA, 1 + 3 * PART, 16, LANES), f32),
            pltpu.VMEM((KA, 1 + 3 * PART, 16, LANES), f32),
            pltpu.VMEM((2, KA, PART, 6, 8, LANES), f32),
            pltpu.VMEM((512, 256), jnp.bfloat16),
            *[pltpu.VMEM((2, ALL_ROWS, 6, 8, LANES), f32)] * 5,
            pltpu.VMEM((2, 2, 8, 6, 8, LANES), f32),
            pltpu.VMEM((2, 2, 8, 6, 8, LANES), f32),
            pltpu.VMEM((2, 2, 6, 8, LANES), f32),
            pltpu.VMEM((2, 4, 6, 8, LANES), f32),
            pltpu.VMEM((8, 8, LANES), jnp.int32),
            pltpu.VMEM((2, 8, LANES), jnp.int32),
            pltpu.VMEM((2, 8, 8, LANES), f32),
            pltpu.VMEM((8, 64, LANES), f32),
            pltpu.VMEM((2, 64, 7, 8, LANES), f32),
            pltpu.VMEM((2, 5, 8, LANES), f32),
            dma((KA,)),
            dma((KA,)),
            dma((2, KA)),
            dma((2, KA)),
            dma((2, 8)),
            dma((2, 8)),
            dma((4,)),
            dma((4,)),
        ],
        compiler_params=pltpu.CompilerParams(
            collective_id=0, has_side_effects=True, vmem_limit_bytes=48 * 2**20
        ),
        name="adjoint",
    )(loads.reshape(16 * 3 * ROWS, LANES), sleeper_pos, material, material_table)
    return result.reshape(16, 2, 3, ROWS, LANES)


def solution(mesh):
    return jax.shard_map(
        local,
        mesh=mesh,
        in_specs=(P("ka", None, "gy", "gz"), P("ka"), P("gy", "gz"), P()),
        out_specs=P("ka", None, None, "gy", "gz"),
        check_vma=False,
    )
```

```python
import math

import jax
import jax.numpy as jnp
from jax import lax
from jax.experimental import pallas as pl
from jax.experimental.pallas import tpu as pltpu
from jax.sharding import PartitionSpec as P

KW = 128
NMAT = 8
KA, GY, GZ = 8, 8, 4
LANES = 128
ROWS = 32
PART = ROWS // KA
STEPS = 7
STRIP = 21
TOP, LEFT, RIGHT, ALL_ROWS = 8, 49, 59, 68
MESH = pl.DeviceIdType.MESH
f32 = jnp.float32


def sine(angle):
    square = angle * angle
    value = jnp.full_like(angle, 1.0 / math.factorial(13))
    for degree in (11, 9, 7, 5, 3, 1):
        sign = -1.0 if (degree // 2) % 2 else 1.0
        value = value * square + sign / math.factorial(degree)
    return value * angle


def kernel(
    loads_hbm, pos_hbm, material_hbm, table_hbm, out,
    loads, pos, table, s1, r1, s2, wm, f_b, f_a, f_c, f_u, f_r, f_o,
    strip_out, strip_in, corner_out, corner_in, mat, mat_in, mask, cells, coupling, per_k,
    p1_send, p1_recv, p2_send, p2_recv, halo_send, halo_recv, mat_send, mat_recv, in_sem,
):
    ka, gy, gz = lax.axis_index("ka"), lax.axis_index("gy"), lax.axis_index("gz")
    shape = (8, LANES)
    sub = lax.broadcasted_iota(jnp.int32, shape, 0)
    lane = lax.broadcasted_iota(jnp.int32, shape, 1)

    barrier = pltpu.get_barrier_semaphore()
    for o in range(1, KA):
        pl.semaphore_signal(
            barrier, inc=1, device_id={"ka": (ka + o) % KA}, device_id_type=MESH
        )
    for dy in (-1, 0, 1):
        for dz in (-1, 0, 1):
            if dy or dz:
                pl.semaphore_signal(
                    barrier,
                    inc=1,
                    device_id={"gy": (gy + dy + GY) % GY, "gz": (gz + dz + GZ) % GZ},
                    device_id_type=MESH,
                )

    arguments = [
        pltpu.make_async_copy(src, dst, in_sem.at[n])
        for n, (src, dst) in enumerate(
            (
                (pos_hbm, pos),
                (loads_hbm, loads),
                (material_hbm, mat.at[pl.ds(1, ROWS // 8)]),
                (table_hbm, table),
            )
        )
    ]
    for copy in arguments:
        copy.start()
    arguments[0].wait()

    position = jnp.zeros(shape, jnp.int32)
    for s in range(16):
        position = jnp.where(lane == ka * 16 + s, pos[s], position)
    position = position.astype(f32)
    arguments[1].wait()

    def stage(o, carry):
        first = ((ka + o) % KA) * PART
        s1[o, 0:8, :] = position
        for h in range(2):
            for yy in range(PART):
                for comp in range(3):
                    start = h * 8 * 96 + comp * ROWS + first + yy
                    at = 8 + (yy * 3 + comp) * 16 + h * 8
                    s1[o, at : at + 8, :] = loads[pl.ds(start, 8, stride=96), :]
        return carry

    lax.fori_loop(0, KA, stage, 0)
    zero = jnp.zeros(shape, f32)

    def clear_rows(first):
        def body(row, carry):
            for buffer in (f_b, f_a, f_c, f_u, f_r):
                for g in range(2):
                    for c in range(6):
                        buffer[g, row, c] = zero
            return carry

        lax.fori_loop(first, first + 8, body, 0)

    pl.when(gy == 0)(lambda: clear_rows(0))
    pl.when(gy == GY - 1)(lambda: clear_rows(TOP + ROWS))
    arguments[2].wait()
    arguments[3].wait()

    pl.semaphore_wait(barrier, KA - 1 + 8)

    exists = {-1: gy > 0, 1: gy < GY - 1}, {-1: gz > 0, 1: gz < GZ - 1}

    def send(src, dst, dy, dz, sends, recvs, at):
        copy = pltpu.make_async_remote_copy(
            src_ref=src,
            dst_ref=dst,
            send_sem=sends.at[at],
            recv_sem=recvs.at[at],
            device_id={"gy": (gy + dy + GY) % GY, "gz": (gz + dz + GZ) % GZ},
            device_id_type=MESH,
        )
        to, origin = True, True
        if dy:
            to, origin = exists[0][dy], exists[0][-dy]
        if dz:
            to = exists[1][dz] if to is True else jnp.logical_and(to, exists[1][dz])
            origin = exists[1][-dz] if origin is True else jnp.logical_and(origin, exists[1][-dz])
        return copy, to, origin

    def start(message):
        pl.when(message[1])(lambda: message[0].start())

    def finish(message):
        pl.when(message[1])(lambda: message[0].wait_send())

    def receive(message):
        pl.when(message[2])(lambda: message[0].wait_recv())

    mat_rows = (
        send(mat.at[1], mat.at[5], -1, 0, mat_send, mat_recv, 0),
        send(mat.at[4], mat.at[0], 1, 0, mat_send, mat_recv, 1),
    )
    mat_strips = (
        send(mat.at[6], mat_in.at[0], 0, 1, mat_send, mat_recv, 2),
        send(mat.at[7], mat_in.at[1], 0, -1, mat_send, mat_recv, 3),
    )
    for message in mat_rows:
        start(message)

    def copy1(o):
        return pltpu.make_async_remote_copy(
            src_ref=s1.at[o],
            dst_ref=r1.at[ka],
            send_sem=p1_send.at[o],
            recv_sem=p1_recv.at[o],
            device_id={"ka": (ka + o) % KA},
            device_id_type=MESH,
        )

    def arrival1(o):
        return pltpu.make_async_remote_copy(
            src_ref=s1.at[o],
            dst_ref=r1.at[(ka + KA - o) % KA],
            send_sem=p1_send.at[o],
            recv_sem=p1_recv.at[o],
            device_id={"ka": (ka + o) % KA},
            device_id_type=MESH,
        )

    for o in (4, 3, 5, 2, 6, 1, 7):
        copy1(o).start()
    r1[ka] = s1[0]

    block = lane // STRIP
    place = lane - block * STRIP
    for message in mat_rows:
        receive(message)
    for side in range(2):
        value = mat[5]
        value = pltpu.roll(value, (STRIP * 5 + 7 + 7 * side) % LANES, 1)
        for j in range(5):
            value = jnp.where(block == j, pltpu.roll(mat[j], STRIP * j + 7 + 7 * side, 1), value)
        mat[6 + side] = value
    for message in mat_strips:
        start(message)

    for side in range(2):
        row = gy * ROWS + 8 * block - 8
        column = gz * LANES + place + (LANES - 14 if side else -7)
        inside = jnp.logical_and(column >= 0, column < GZ * LANES)
        inside = jnp.logical_and(inside, block < 6)
        for i in range(8):
            valid = jnp.logical_and(row + i >= 0, row + i < GY * ROWS)
            if i == 0:
                valid = jnp.logical_and(valid, block > 0)
            if i == 7:
                valid = jnp.logical_and(valid, block < 5)
            mask[side, i] = jnp.where(jnp.logical_and(inside, valid), 1.0, 0.0)

    squares, centers = [], []
    for g in range(2):
        k = ka * 16 + g * 8 + sub
        half_turn = jnp.minimum(k, KW - k).astype(f32) * (math.pi / KW)
        root = 2.0 * sine(half_turn)
        q = root * root
        low, high = None, None
        for m in range(NMAT):
            entry = [jnp.full(shape, table[m, f], f32) for f in range(7)]
            off = [jnp.abs(entry[f]) for f in (4, 5, 6)]
            sums = (off[0] + off[1], off[0] + off[2], off[1] + off[2])
            lo = [entry[1 + c] - sums[c] for c in range(3)]
            hi = [entry[1 + c] + sums[c] for c in range(3)]
            lo = entry[0] + jnp.minimum(jnp.minimum(lo[0], lo[1]), lo[2]) * q
            hi = entry[0] + jnp.maximum(jnp.maximum(hi[0], hi[1]), hi[2]) * q
            low = lo if low is None else jnp.minimum(low, lo)
            high = hi if high is None else jnp.maximum(high, hi)
        high = 8.0 + high
        center = 0.5 * (high + low)
        width = 0.5 * (high - low)
        ratio = center / width
        weight = 1.0 / ratio
        d = [1.0 / center]
        r = [jnp.ones(shape, f32)]
        u = list(d)
        for _ in range(3):
            r = r + [zero]
            lowered = [center * d[j] if j < len(d) else zero for j in range(len(r))]
            raised = [zero] + d
            r = [r[j] - lowered[j] + raised[j] for j in range(len(r))]
            new_weight = 1.0 / (2.0 * ratio - weight)
            d = [
                (new_weight * weight) * (d[j] if j < len(d) else zero)
                + (2.0 * new_weight / width) * r[j]
                for j in range(len(r))
            ]
            u = [(u[j] if j < len(u) else zero) + d[j] for j in range(len(d))]
            weight = new_weight
        for j in range(4):
            per_k[g, j] = u[j]
        per_k[g, 4] = center
        squares.append(q)
        centers.append(center)

    for message in mat_strips:
        receive(message)
    foreign = (place < 7, place >= 14)
    mat_strip = [jnp.where(foreign[side], mat_in[side], mat[6 + side]) for side in range(2)]

    def gather_cells(t, carry):
        index = mat[t]
        rows = pl.ds(pl.multiple_of(t * 8, 8), 8)
        for f in range(8):
            value = jnp.zeros(shape, f32)
            for m in range(NMAT):
                value = jnp.where(index == m, table[m, f], value)
            cells[f, rows, :] = value
        return carry

    lax.fori_loop(0, 6, gather_cells, 0)
    for side in range(2):
        for f in range(8):
            value = jnp.zeros(shape, f32)
            for m in range(NMAT):
                value = jnp.where(mat_strip[side] == m, table[m, f], value)
            cells[f, 48 + 8 * side : 56 + 8 * side, :] = value

    def prepare_coupling(y, carry):
        row = [cells[f, pl.ds(y, 1), :] for f in range(8)]
        for g in range(2):
            q = squares[g]
            base = centers[g] - 4.0 - row[0]
            for c in range(3):
                coupling[g, y, c] = base - q * row[1 + c]
                coupling[g, y, 3 + c] = -(q * row[4 + c])
            coupling[g, y, 6] = q * row[7]
        return carry

    lax.fori_loop(0, 64, prepare_coupling, 0)

    for o in range(1, KA):
        arrival1(o).wait_recv()
    positions = r1[0, 0:1, :]
    for i in range(1, KA):
        positions += r1[i, 0:1, :]
    positions = jnp.broadcast_to(positions, (256, LANES)).astype(jnp.int32)
    wide = (256, LANES)
    row_no = lax.broadcasted_iota(jnp.int32, wide, 0)
    k_of = (row_no // 16) * 8 + row_no % 8
    imaginary = (row_no // 8) % 2
    turn = (k_of * positions + 32 * imaginary) & (KW - 1)
    away = jnp.abs(turn - KW // 2) - KW // 4
    weights = sine(away.astype(f32) * (2.0 * math.pi / KW))
    w_hi = weights.astype(jnp.bfloat16)
    w_lo = (weights - w_hi.astype(f32)).astype(jnp.bfloat16)
    wm[0:256, 0:128] = w_hi
    wm[0:256, 128:256] = w_hi
    wm[256:512, 0:128] = w_lo
    wm[256:512, 128:256] = jnp.zeros((256, 128), jnp.bfloat16)

    def transform(yy, carry):
        for comp in range(3):
            row = pl.ds(pl.multiple_of(8 + (yy * 3 + comp) * 16, 8), 16)
            values = jnp.concatenate([r1[i, row, :] for i in range(KA)], axis=0)
            v_hi = values.astype(jnp.bfloat16)
            v_lo = (values - v_hi.astype(f32)).astype(jnp.bfloat16)
            product = jnp.dot(
                wm[...], jnp.concatenate([v_hi, v_lo], axis=0), preferred_element_type=f32
            )
            product = product[0:256] + product[256:512]
            for d in range(KA):
                for g in range(2):
                    for ri in range(2):
                        at = ((d * 2 + g) * 2 + ri) * 8
                        s2[g, d, yy, ri * 3 + comp] = product[at : at + 8]
        return carry

    lax.fori_loop(0, PART, transform, 0)

    def copy2(g, o):
        return pltpu.make_async_remote_copy(
            src_ref=s2.at[g, (ka + o) % KA],
            dst_ref=f_b.at[g, pl.ds(TOP + PART * ka, PART)],
            send_sem=p2_send.at[g, o],
            recv_sem=p2_recv.at[g, o],
            device_id={"ka": (ka + o) % KA},
            device_id_type=MESH,
        )

    def arrival2(g, o):
        return pltpu.make_async_remote_copy(
            src_ref=s2.at[g, (ka + o) % KA],
            dst_ref=f_b.at[g, pl.ds(TOP + PART * ((ka + KA - o) % KA), PART)],
            send_sem=p2_send.at[g, o],
            recv_sem=p2_recv.at[g, o],
            device_id={"ka": (ka + o) % KA},
            device_id_type=MESH,
        )

    far_first = (4, 3, 5, 2, 6, 1, 7)
    for o in far_first:
        copy2(0, o).start()
    for g in range(2):
        f_b[g, pl.ds(TOP + PART * ka, PART)] = s2[g, ka]
    for o in far_first:
        copy2(0, o).wait_send()
        copy2(1, o).start()

    def messages(g):
        rows = (
            send(f_b.at[g, pl.ds(TOP, 7)], f_b.at[g, pl.ds(TOP + ROWS, 7)], -1, 0, halo_send, halo_recv, (g, 0)),
            send(f_b.at[g, pl.ds(TOP + ROWS - 7, 7)], f_b.at[g, pl.ds(1, 7)], 1, 0, halo_send, halo_recv, (g, 1)),
        )
        sides = (
            send(strip_out.at[g, 0], strip_in.at[g, 0], 0, 1, halo_send, halo_recv, (g, 2)),
            send(strip_out.at[g, 1], strip_in.at[g, 1], 0, -1, halo_send, halo_recv, (g, 3)),
        )
        corners = tuple(
            send(corner_out.at[g, n // 2], corner_in.at[g, n], dy, dz, halo_send, halo_recv, (g, 4 + n))
            for n, (dy, dz) in enumerate(((1, 1), (1, -1), (-1, 1), (-1, -1)))
        )
        return rows, sides + corners

    def exchange(g):
        for o in far_first:
            arrival2(g, o).wait_recv()
        rows, others = messages(g)
        for message in rows:
            start(message)

        def body(c, carry):
            near = [zero, zero]
            for i in range(8):
                values = [f_b[g, TOP + 8 * j + i, c] for j in range(4)]
                for side in range(2):
                    shift = 7 + 7 * side
                    strip = pltpu.roll(values[3], (STRIP * 4 + shift) % LANES, 1)
                    for j in (2, 1, 0):
                        strip = jnp.where(
                            block <= j + 1, pltpu.roll(values[j], STRIP * (j + 1) + shift, 1), strip
                        )
                    strip_out[g, side, i, c] = strip
                here = jnp.logical_and(lane >= 14 * i, lane < 14 * i + 14)
                near[0] = jnp.where(here, pltpu.roll(values[3], 14 * i + 7, 1), near[0])
                near[1] = jnp.where(here, pltpu.roll(values[0], 14 * i + 7, 1), near[1])
            corner_out[g, 0, c] = near[0]
            corner_out[g, 1, c] = near[1]
            return carry

        lax.fori_loop(0, 6, body, 0, unroll=2)
        for message in others:
            start(message)

    inner_block = jnp.logical_and(block >= 1, block <= 4)

    def wrap_strips(buffer, g, c):
        for first in (LEFT, RIGHT):
            buffer[g, first - 1, c] = pltpu.roll(buffer[g, first + 7, c], STRIP, 1)
            buffer[g, first + 8, c] = pltpu.roll(buffer[g, first, c], LANES - STRIP, 1)

    def assemble(g):
        masks = [[mask[side, i] > 0.5 for i in range(8)] for side in range(2)]

        def body(c, carry):
            for i in range(8):
                above, below = f_b[g, i, c], f_b[g, TOP + ROWS + i, c]
                for side in range(2):
                    shift = 7 + 7 * side
                    own = jnp.where(
                        block == 0,
                        pltpu.roll(above, shift, 1),
                        jnp.where(
                            block == 5,
                            pltpu.roll(below, (STRIP * 5 + shift) % LANES, 1),
                            strip_out[g, side, i, c],
                        ),
                    )
                    lower = 2 * LANES + 7 * side - 14 * i
                    other = jnp.where(
                        block == 0,
                        pltpu.roll(corner_in[g, side, c], lower % LANES, 1),
                        jnp.where(
                            block == 5,
                            pltpu.roll(corner_in[g, 2 + side, c], (lower + STRIP * 5) % LANES, 1),
                            strip_in[g, side, i, c],
                        ),
                    )
                    value = jnp.where(foreign[side], other, own)
                    f_b[g, (LEFT, RIGHT)[side] + i, c] = jnp.where(masks[side][i], value, 0.0)
            return carry

        lax.fori_loop(0, 6, body, 0, unroll=2)
        for c in range(6):
            wrap_strips(f_b, g, c)

    source = (f_b, f_a, f_c, f_u, f_r, f_a, f_c)
    target = (f_a, f_c, f_u, f_r, f_a, f_c, f_o)

    def advance(e, g, at, cell, keep=None):
        src = source[e]
        here = [src[g, at, c] for c in range(6)]
        k = [coupling[g, cell, f] for f in range(7)]
        scale = per_k[g, (2, 1, 0, 4, 2, 1, 0)[e]]
        for c in range(6):
            comp, other = c % 3, (c + 3) % 6
            value = src[g, at - 1, c] + src[g, at + 1, c]
            value += pltpu.roll(here[c], 1, 1) + pltpu.roll(here[c], LANES - 1, 1)
            value += k[comp] * here[c]
            for j in range(3):
                if j != comp:
                    value += k[2 + comp + j] * here[c - comp + j]
            if c < 3:
                value += k[6] * here[other]
            else:
                value -= k[6] * here[other]
            if e in (0, 4):
                value = per_k[g, 3] * value + scale * here[c]
            elif e in (1, 2):
                value += scale * f_b[g, at, c]
            elif e == 3:
                value = f_b[g, at, c] + (value - scale * here[c])
            else:
                value += scale * f_r[g, at, c]
            if e == 6:
                value += f_u[g, at, c]
            if keep is not None:
                value *= keep
            target[e][g, at, c] = value

    def main_rows(e, g, first, count, unroll):
        def body(i, carry):
            advance(e, g, i + first, i + first)
            return carry

        lax.fori_loop(0, count, body, 0, unroll=unroll)

    def interior(g):
        for e in range(STEPS):
            main_rows(e, g, TOP + e + 1, 30 - 2 * e, (15, 14, 13, 12, 11, 10, 9)[e])

    def borders_and_strips(g):
        above = jnp.where(gy > 0, 1.0, 0.0)
        below = jnp.where(gy < GY - 1, 1.0, 0.0)
        for e in range(STEPS):

            def body(i, carry):
                at = TOP - 6 + e + i
                advance(e, g, at, at, jnp.where(i < 6 - e, above, 1.0))
                at = TOP + ROWS - 2 - e + i
                advance(e, g, at, at, jnp.where(i >= e + 2, below, 1.0))
                advance(e, g, LEFT + i, 48 + i, mask[0, i])
                advance(e, g, RIGHT + i, 56 + i, mask[1, i])
                return carry

            lax.fori_loop(0, 8, body, 0, unroll=8)
            if e < STEPS - 1:
                for c in range(6):
                    wrap_strips(target[e], g, c)

    def deliver(g):
        edge = jnp.logical_or(lane < 7, lane >= LANES - 7)

        def body(i, carry):
            for c in range(6):
                joined = jnp.where(
                    place < 7, pltpu.roll(f_o[g, RIGHT + i, c], LANES - 7, 1), f_o[g, LEFT + i, c]
                )
                for j in range(4):
                    y = 8 * j + i
                    value = jnp.where(
                        edge,
                        pltpu.roll(joined, (2 * LANES - STRIP * (j + 1) - 7) % LANES, 1),
                        f_o[g, TOP + y, c],
                    )
                    out[pl.ds(g * 8 * 192 + c * ROWS + y, 8, stride=192), :] = value
            return carry

        lax.fori_loop(0, 8, body, 0, unroll=4)

    def await_halo(g):
        for group in messages(g):
            for message in group:
                receive(message)

    exchange(0)
    interior(0)
    await_halo(0)
    assemble(0)
    exchange(1)
    borders_and_strips(0)
    deliver(0)
    interior(1)
    await_halo(1)
    assemble(1)
    borders_and_strips(1)
    deliver(1)

    for o in range(1, KA):
        copy1(o).wait_send()
        copy2(1, o).wait_send()
    for message in mat_rows + mat_strips:
        finish(message)
    for g in range(2):
        for group in messages(g):
            for message in group:
                finish(message)


def local(loads, sleeper_pos, material, material_table):
    vmem = pl.BlockSpec(memory_space=pltpu.VMEM)
    hbm = pl.BlockSpec(memory_space=pltpu.HBM)
    dma = pltpu.SemaphoreType.DMA
    result = pl.pallas_call(
        kernel,
        out_shape=jax.ShapeDtypeStruct((16 * 6 * ROWS, LANES), f32),
        in_specs=[hbm] * 4,
        out_specs=vmem,
        scratch_shapes=[
            pltpu.VMEM((16 * 3 * ROWS, LANES), f32),
            pltpu.SMEM((16,), jnp.int32),
            pltpu.SMEM((NMAT, 8), f32),
            pltpu.VMEM((KA, 8 + 3 * PART * 16, LANES), f32),
            pltpu.VMEM((KA, 8 + 3 * PART * 16, LANES), f32),
            pltpu.VMEM((2, KA, PART, 6, 8, LANES), f32),
            pltpu.VMEM((512, 256), jnp.bfloat16),
            *[pltpu.VMEM((2, ALL_ROWS, 6, 8, LANES), f32)] * 6,
            pltpu.VMEM((2, 2, 8, 6, 8, LANES), f32),
            pltpu.VMEM((2, 2, 8, 6, 8, LANES), f32),
            pltpu.VMEM((2, 2, 6, 8, LANES), f32),
            pltpu.VMEM((2, 4, 6, 8, LANES), f32),
            pltpu.VMEM((8, 8, LANES), jnp.int32),
            pltpu.VMEM((2, 8, LANES), jnp.int32),
            pltpu.VMEM((2, 8, 8, LANES), f32),
            pltpu.VMEM((8, 64, LANES), f32),
            pltpu.VMEM((2, 64, 7, 8, LANES), f32),
            pltpu.VMEM((2, 5, 8, LANES), f32),
            dma((KA,)),
            dma((KA,)),
            dma((2, KA)),
            dma((2, KA)),
            dma((2, 8)),
            dma((2, 8)),
            dma((4,)),
            dma((4,)),
            dma((4,)),
        ],
        compiler_params=pltpu.CompilerParams(
            collective_id=0, has_side_effects=True, vmem_limit_bytes=48 * 2**20
        ),
        name="adjoint",
    )(loads.reshape(16 * 3 * ROWS, LANES), sleeper_pos, material.reshape(ROWS // 8, 8, LANES), material_table)
    return result.reshape(16, 2, 3, ROWS, LANES)


def solution(mesh):
    return jax.shard_map(
        local,
        mesh=mesh,
        in_specs=(P("ka", None, "gy", "gz"), P("ka"), P("gy", "gz"), P()),
        out_specs=P("ka", None, None, "gy", "gz"),
        check_vma=False,
    )
```

```python
import math

import jax
import jax.numpy as jnp
from jax import lax
from jax.experimental import pallas as pl
from jax.experimental.pallas import tpu as pltpu
from jax.sharding import PartitionSpec as P

KW = 128
NMAT = 8
KA, GY, GZ = 8, 8, 4
LANES = 128
ROWS = 32
PART = ROWS // KA
STEPS = 7
STRIP = 21
TOP, LEFT, RIGHT, ALL_ROWS = 8, 49, 59, 68
MESH = pl.DeviceIdType.MESH
f32 = jnp.float32


def sine(angle):
    square = angle * angle
    value = jnp.full_like(angle, 1.0 / math.factorial(13))
    for degree in (11, 9, 7, 5, 3, 1):
        sign = -1.0 if (degree // 2) % 2 else 1.0
        value = value * square + sign / math.factorial(degree)
    return value * angle


def kernel(
    loads_hbm, pos_hbm, material_hbm, table_hbm, out,
    loads, pos, table, s1, r1, s2, wm, f_b, f_a, f_c, f_u, f_r, f_o,
    strip_out, strip_in, corner_out, corner_in, mat, mat_in, mask, cells, coupling, per_k,
    p1_send, p1_recv, p2_send, p2_recv, halo_send, halo_recv, mat_send, mat_recv, in_sem,
):
    ka, gy, gz = lax.axis_index("ka"), lax.axis_index("gy"), lax.axis_index("gz")
    shape = (8, LANES)
    sub = lax.broadcasted_iota(jnp.int32, shape, 0)
    lane = lax.broadcasted_iota(jnp.int32, shape, 1)

    barrier = pltpu.get_barrier_semaphore()
    for o in range(1, KA):
        pl.semaphore_signal(
            barrier, inc=1, device_id={"ka": (ka + o) % KA}, device_id_type=MESH
        )
    for dy in (-1, 0, 1):
        for dz in (-1, 0, 1):
            if dy or dz:
                pl.semaphore_signal(
                    barrier,
                    inc=1,
                    device_id={"gy": (gy + dy + GY) % GY, "gz": (gz + dz + GZ) % GZ},
                    device_id_type=MESH,
                )

    arguments = [
        pltpu.make_async_copy(src, dst, in_sem.at[n])
        for n, (src, dst) in enumerate(
            (
                (pos_hbm, pos),
                (loads_hbm, loads),
                (material_hbm, mat.at[pl.ds(1, ROWS // 8)]),
                (table_hbm, table),
            )
        )
    ]
    for copy in arguments:
        copy.start()
    arguments[0].wait()

    position = jnp.zeros(shape, jnp.int32)
    for s in range(16):
        position = jnp.where(lane == ka * 16 + s, pos[s], position)
    position = position.astype(f32)
    arguments[1].wait()

    def stage(o, carry):
        first = ((ka + o) % KA) * PART
        s1[o, 0:8, :] = position
        for h in range(2):
            for yy in range(PART):
                for comp in range(3):
                    start = h * 8 * 96 + comp * ROWS + first + yy
                    at = 8 + (yy * 3 + comp) * 16 + h * 8
                    s1[o, at : at + 8, :] = loads[pl.ds(start, 8, stride=96), :]
        return carry

    lax.fori_loop(0, KA, stage, 0)
    zero = jnp.zeros(shape, f32)

    def clear_rows(first):
        def body(row, carry):
            for buffer in (f_b, f_a, f_c, f_u, f_r):
                for g in range(2):
                    for c in range(6):
                        buffer[g, row, c] = zero
            return carry

        lax.fori_loop(first, first + 8, body, 0)

    pl.when(gy == 0)(lambda: clear_rows(0))
    pl.when(gy == GY - 1)(lambda: clear_rows(TOP + ROWS))
    arguments[2].wait()
    arguments[3].wait()

    pl.semaphore_wait(barrier, KA - 1 + 8)

    exists = {-1: gy > 0, 1: gy < GY - 1}, {-1: gz > 0, 1: gz < GZ - 1}

    def send(src, dst, dy, dz, sends, recvs, at):
        copy = pltpu.make_async_remote_copy(
            src_ref=src,
            dst_ref=dst,
            send_sem=sends.at[at],
            recv_sem=recvs.at[at],
            device_id={"gy": (gy + dy + GY) % GY, "gz": (gz + dz + GZ) % GZ},
            device_id_type=MESH,
        )
        to, origin = True, True
        if dy:
            to, origin = exists[0][dy], exists[0][-dy]
        if dz:
            to = exists[1][dz] if to is True else jnp.logical_and(to, exists[1][dz])
            origin = exists[1][-dz] if origin is True else jnp.logical_and(origin, exists[1][-dz])
        return copy, to, origin

    def start(message):
        pl.when(message[1])(lambda: message[0].start())

    def finish(message):
        pl.when(message[1])(lambda: message[0].wait_send())

    def receive(message):
        pl.when(message[2])(lambda: message[0].wait_recv())

    mat_rows = (
        send(mat.at[1], mat.at[5], -1, 0, mat_send, mat_recv, 0),
        send(mat.at[4], mat.at[0], 1, 0, mat_send, mat_recv, 1),
    )
    mat_strips = (
        send(mat.at[6], mat_in.at[0], 0, 1, mat_send, mat_recv, 2),
        send(mat.at[7], mat_in.at[1], 0, -1, mat_send, mat_recv, 3),
    )
    for message in mat_rows:
        start(message)

    early, late = pl.ds(0, 8 + PART * 24), pl.ds(8 + PART * 24, PART * 24)

    def copy1(part, o, source):
        rows = late if part else early
        return pltpu.make_async_remote_copy(
            src_ref=s1.at[o, rows],
            dst_ref=r1.at[source, rows],
            send_sem=p1_send.at[part, o],
            recv_sem=p1_recv.at[part, o],
            device_id={"ka": (ka + o) % KA},
            device_id_type=MESH,
        )

    far_first = (4, 3, 5, 2, 6, 1, 7)
    for o in far_first:
        copy1(0, o, ka).start()
    r1[ka] = s1[0]

    block = lane // STRIP
    place = lane - block * STRIP
    for message in mat_rows:
        receive(message)
    for side in range(2):
        value = mat[5]
        value = pltpu.roll(value, (STRIP * 5 + 7 + 7 * side) % LANES, 1)
        for j in range(5):
            value = jnp.where(block == j, pltpu.roll(mat[j], STRIP * j + 7 + 7 * side, 1), value)
        mat[6 + side] = value
    for message in mat_strips:
        start(message)

    for side in range(2):
        row = gy * ROWS + 8 * block - 8
        column = gz * LANES + place + (LANES - 14 if side else -7)
        inside = jnp.logical_and(column >= 0, column < GZ * LANES)
        inside = jnp.logical_and(inside, block < 6)
        for i in range(8):
            valid = jnp.logical_and(row + i >= 0, row + i < GY * ROWS)
            if i == 0:
                valid = jnp.logical_and(valid, block > 0)
            if i == 7:
                valid = jnp.logical_and(valid, block < 5)
            mask[side, i] = jnp.where(jnp.logical_and(inside, valid), 1.0, 0.0)

    squares, centers = [], []
    for g in range(2):
        k = ka * 16 + g * 8 + sub
        half_turn = jnp.minimum(k, KW - k).astype(f32) * (math.pi / KW)
        root = 2.0 * sine(half_turn)
        q = root * root
        low, high = None, None
        for m in range(NMAT):
            entry = [jnp.full(shape, table[m, f], f32) for f in range(7)]
            off = [jnp.abs(entry[f]) for f in (4, 5, 6)]
            sums = (off[0] + off[1], off[0] + off[2], off[1] + off[2])
            lo = [entry[1 + c] - sums[c] for c in range(3)]
            hi = [entry[1 + c] + sums[c] for c in range(3)]
            lo = entry[0] + jnp.minimum(jnp.minimum(lo[0], lo[1]), lo[2]) * q
            hi = entry[0] + jnp.maximum(jnp.maximum(hi[0], hi[1]), hi[2]) * q
            low = lo if low is None else jnp.minimum(low, lo)
            high = hi if high is None else jnp.maximum(high, hi)
        high = 8.0 + high
        center = 0.5 * (high + low)
        width = 0.5 * (high - low)
        ratio = center / width
        weight = 1.0 / ratio
        d = [1.0 / center]
        r = [jnp.ones(shape, f32)]
        u = list(d)
        for _ in range(3):
            r = r + [zero]
            lowered = [center * d[j] if j < len(d) else zero for j in range(len(r))]
            raised = [zero] + d
            r = [r[j] - lowered[j] + raised[j] for j in range(len(r))]
            new_weight = 1.0 / (2.0 * ratio - weight)
            d = [
                (new_weight * weight) * (d[j] if j < len(d) else zero)
                + (2.0 * new_weight / width) * r[j]
                for j in range(len(r))
            ]
            u = [(u[j] if j < len(u) else zero) + d[j] for j in range(len(d))]
            weight = new_weight
        for j in range(4):
            per_k[g, j] = u[j]
        per_k[g, 4] = center
        squares.append(q)
        centers.append(center)

    for o in far_first:
        copy1(0, o, ka).wait_send()
        copy1(1, o, ka).start()

    for message in mat_strips:
        receive(message)
    foreign = (place < 7, place >= 14)
    mat_strip = [jnp.where(foreign[side], mat_in[side], mat[6 + side]) for side in range(2)]

    def gather_cells(t, carry):
        index = mat[t]
        rows = pl.ds(pl.multiple_of(t * 8, 8), 8)
        for f in range(8):
            value = jnp.zeros(shape, f32)
            for m in range(NMAT):
                value = jnp.where(index == m, table[m, f], value)
            cells[f, rows, :] = value
        return carry

    lax.fori_loop(0, 6, gather_cells, 0)
    for side in range(2):
        for f in range(8):
            value = jnp.zeros(shape, f32)
            for m in range(NMAT):
                value = jnp.where(mat_strip[side] == m, table[m, f], value)
            cells[f, 48 + 8 * side : 56 + 8 * side, :] = value

    def prepare_coupling(y, carry):
        row = [cells[f, pl.ds(y, 1), :] for f in range(8)]
        for g in range(2):
            q = squares[g]
            base = centers[g] - 4.0 - row[0]
            for c in range(3):
                coupling[g, y, c] = base - q * row[1 + c]
                coupling[g, y, 3 + c] = -(q * row[4 + c])
            coupling[g, y, 6] = q * row[7]
        return carry

    lax.fori_loop(0, 64, prepare_coupling, 0)

    for o in range(1, KA):
        copy1(0, o, (ka + KA - o) % KA).wait_recv()
    positions = r1[0, 0:1, :]
    for i in range(1, KA):
        positions += r1[i, 0:1, :]
    positions = jnp.broadcast_to(positions, (256, LANES)).astype(jnp.int32)
    wide = (256, LANES)
    row_no = lax.broadcasted_iota(jnp.int32, wide, 0)
    k_of = (row_no // 16) * 8 + row_no % 8
    imaginary = (row_no // 8) % 2
    turn = (k_of * positions + 32 * imaginary) & (KW - 1)
    away = jnp.abs(turn - KW // 2) - KW // 4
    weights = sine(away.astype(f32) * (2.0 * math.pi / KW))
    w_hi = weights.astype(jnp.bfloat16)
    w_lo = (weights - w_hi.astype(f32)).astype(jnp.bfloat16)
    wm[0:256, 0:128] = w_hi
    wm[0:256, 128:256] = w_hi
    wm[256:512, 0:128] = w_lo
    wm[256:512, 128:256] = jnp.zeros((256, 128), jnp.bfloat16)

    def transform(yy, carry):
        for comp in range(3):
            row = pl.ds(pl.multiple_of(8 + (yy * 3 + comp) * 16, 8), 16)
            values = jnp.concatenate([r1[i, row, :] for i in range(KA)], axis=0)
            v_hi = values.astype(jnp.bfloat16)
            v_lo = (values - v_hi.astype(f32)).astype(jnp.bfloat16)
            product = jnp.dot(
                wm[...], jnp.concatenate([v_hi, v_lo], axis=0), preferred_element_type=f32
            )
            product = product[0:256] + product[256:512]
            for d in range(KA):
                for g in range(2):
                    for ri in range(2):
                        at = ((d * 2 + g) * 2 + ri) * 8
                        s2[g, d, yy, ri * 3 + comp] = product[at : at + 8]
        return carry

    first_row = (0, PART // 2, 0)
    row_count = (PART // 2, PART // 2, PART)

    def copy2(part, o, source):
        g, first, count = part // 2, first_row[part], row_count[part]
        return pltpu.make_async_remote_copy(
            src_ref=s2.at[g, (ka + o) % KA, pl.ds(first, count)],
            dst_ref=f_b.at[g, pl.ds(TOP + PART * source + first, count)],
            send_sem=p2_send.at[part, o],
            recv_sem=p2_recv.at[part, o],
            device_id={"ka": (ka + o) % KA},
            device_id_type=MESH,
        )

    lax.fori_loop(0, PART // 2, transform, 0)
    for o in far_first:
        copy2(0, o, ka).start()
    for o in range(1, KA):
        copy1(1, o, (ka + KA - o) % KA).wait_recv()
    lax.fori_loop(PART // 2, PART, transform, 0)
    for o in far_first:
        copy2(1, o, ka).start()
    for g in range(2):
        f_b[g, pl.ds(TOP + PART * ka, PART)] = s2[g, ka]
    for o in far_first:
        copy2(0, o, ka).wait_send()
    for o in far_first:
        copy2(1, o, ka).wait_send()
        copy2(2, o, ka).start()

    def messages(g):
        rows = (
            send(f_b.at[g, pl.ds(TOP, 7)], f_b.at[g, pl.ds(TOP + ROWS, 7)], -1, 0, halo_send, halo_recv, (g, 0)),
            send(f_b.at[g, pl.ds(TOP + ROWS - 7, 7)], f_b.at[g, pl.ds(1, 7)], 1, 0, halo_send, halo_recv, (g, 1)),
        )
        sides = (
            send(strip_out.at[g, 0], strip_in.at[g, 0], 0, 1, halo_send, halo_recv, (g, 2)),
            send(strip_out.at[g, 1], strip_in.at[g, 1], 0, -1, halo_send, halo_recv, (g, 3)),
        )
        corners = tuple(
            send(corner_out.at[g, n // 2], corner_in.at[g, n], dy, dz, halo_send, halo_recv, (g, 4 + n))
            for n, (dy, dz) in enumerate(((1, 1), (1, -1), (-1, 1), (-1, -1)))
        )
        return rows, sides + corners

    def exchange(g):
        for part in (2,) if g else (0, 1):
            for o in far_first:
                copy2(part, o, (ka + KA - o) % KA).wait_recv()
        rows, others = messages(g)
        for message in rows:
            start(message)

        def body(c, carry):
            near = [zero, zero]
            for i in range(8):
                values = [f_b[g, TOP + 8 * j + i, c] for j in range(4)]
                for side in range(2):
                    shift = 7 + 7 * side
                    strip = pltpu.roll(values[3], (STRIP * 4 + shift) % LANES, 1)
                    for j in (2, 1, 0):
                        strip = jnp.where(
                            block <= j + 1, pltpu.roll(values[j], STRIP * (j + 1) + shift, 1), strip
                        )
                    strip_out[g, side, i, c] = strip
                here = jnp.logical_and(lane >= 14 * i, lane < 14 * i + 14)
                near[0] = jnp.where(here, pltpu.roll(values[3], 14 * i + 7, 1), near[0])
                near[1] = jnp.where(here, pltpu.roll(values[0], 14 * i + 7, 1), near[1])
            corner_out[g, 0, c] = near[0]
            corner_out[g, 1, c] = near[1]
            return carry

        lax.fori_loop(0, 6, body, 0, unroll=2)
        for message in others:
            start(message)

    inner_block = jnp.logical_and(block >= 1, block <= 4)

    def wrap_strips(buffer, g, c):
        for first in (LEFT, RIGHT):
            buffer[g, first - 1, c] = pltpu.roll(buffer[g, first + 7, c], STRIP, 1)
            buffer[g, first + 8, c] = pltpu.roll(buffer[g, first, c], LANES - STRIP, 1)

    def assemble(g):
        masks = [[mask[side, i] > 0.5 for i in range(8)] for side in range(2)]

        def body(c, carry):
            for i in range(8):
                above, below = f_b[g, i, c], f_b[g, TOP + ROWS + i, c]
                for side in range(2):
                    shift = 7 + 7 * side
                    own = jnp.where(
                        block == 0,
                        pltpu.roll(above, shift, 1),
                        jnp.where(
                            block == 5,
                            pltpu.roll(below, (STRIP * 5 + shift) % LANES, 1),
                            strip_out[g, side, i, c],
                        ),
                    )
                    lower = 2 * LANES + 7 * side - 14 * i
                    other = jnp.where(
                        block == 0,
                        pltpu.roll(corner_in[g, side, c], lower % LANES, 1),
                        jnp.where(
                            block == 5,
                            pltpu.roll(corner_in[g, 2 + side, c], (lower + STRIP * 5) % LANES, 1),
                            strip_in[g, side, i, c],
                        ),
                    )
                    value = jnp.where(foreign[side], other, own)
                    f_b[g, (LEFT, RIGHT)[side] + i, c] = jnp.where(masks[side][i], value, 0.0)
            return carry

        lax.fori_loop(0, 6, body, 0, unroll=2)
        for c in range(6):
            wrap_strips(f_b, g, c)

    source = (f_b, f_a, f_c, f_u, f_r, f_a, f_c)
    target = (f_a, f_c, f_u, f_r, f_a, f_c, f_o)

    def advance(e, g, at, cell, keep=None):
        src = source[e]
        here = [src[g, at, c] for c in range(6)]
        k = [coupling[g, cell, f] for f in range(7)]
        scale = per_k[g, (2, 1, 0, 4, 2, 1, 0)[e]]
        for c in range(6):
            comp, other = c % 3, (c + 3) % 6
            value = src[g, at - 1, c] + src[g, at + 1, c]
            value += pltpu.roll(here[c], 1, 1) + pltpu.roll(here[c], LANES - 1, 1)
            value += k[comp] * here[c]
            for j in range(3):
                if j != comp:
                    value += k[2 + comp + j] * here[c - comp + j]
            if c < 3:
                value += k[6] * here[other]
            else:
                value -= k[6] * here[other]
            if e in (0, 4):
                value = per_k[g, 3] * value + scale * here[c]
            elif e in (1, 2):
                value += scale * f_b[g, at, c]
            elif e == 3:
                value = f_b[g, at, c] + (value - scale * here[c])
            else:
                value += scale * f_r[g, at, c]
            if e == 6:
                value += f_u[g, at, c]
            if keep is not None:
                value *= keep
            target[e][g, at, c] = value

    def main_rows(e, g, first, count, unroll):
        def body(i, carry):
            advance(e, g, i + first, i + first)
            return carry

        lax.fori_loop(0, count, body, 0, unroll=unroll)

    def interior(g):
        for e in range(STEPS):
            main_rows(e, g, TOP + e + 1, 30 - 2 * e, (15, 14, 13, 12, 11, 10, 9)[e])

    def borders_and_strips(g):
        above = jnp.where(gy > 0, 1.0, 0.0)
        below = jnp.where(gy < GY - 1, 1.0, 0.0)
        for e in range(STEPS):

            def body(i, carry):
                at = TOP - 6 + e + i
                advance(e, g, at, at, jnp.where(i < 6 - e, above, 1.0))
                at = TOP + ROWS - 2 - e + i
                advance(e, g, at, at, jnp.where(i >= e + 2, below, 1.0))
                advance(e, g, LEFT + i, 48 + i, mask[0, i])
                advance(e, g, RIGHT + i, 56 + i, mask[1, i])
                return carry

            lax.fori_loop(0, 8, body, 0, unroll=8)
            if e < STEPS - 1:
                for c in range(6):
                    wrap_strips(target[e], g, c)

    def deliver(g):
        edge = jnp.logical_or(lane < 7, lane >= LANES - 7)

        def body(i, carry):
            for c in range(6):
                joined = jnp.where(
                    place < 7, pltpu.roll(f_o[g, RIGHT + i, c], LANES - 7, 1), f_o[g, LEFT + i, c]
                )
                for j in range(4):
                    y = 8 * j + i
                    value = jnp.where(
                        edge,
                        pltpu.roll(joined, (2 * LANES - STRIP * (j + 1) - 7) % LANES, 1),
                        f_o[g, TOP + y, c],
                    )
                    out[pl.ds(g * 8 * 192 + c * ROWS + y, 8, stride=192), :] = value
            return carry

        lax.fori_loop(0, 8, body, 0, unroll=4)

    def await_halo(g):
        for group in messages(g):
            for message in group:
                receive(message)

    exchange(0)
    interior(0)
    await_halo(0)
    assemble(0)
    exchange(1)
    borders_and_strips(0)
    deliver(0)
    interior(1)
    await_halo(1)
    assemble(1)
    borders_and_strips(1)
    deliver(1)

    for o in range(1, KA):
        copy1(1, o, ka).wait_send()
        copy2(2, o, ka).wait_send()
    for message in mat_rows + mat_strips:
        finish(message)
    for g in range(2):
        for group in messages(g):
            for message in group:
                finish(message)


def local(loads, sleeper_pos, material, material_table):
    vmem = pl.BlockSpec(memory_space=pltpu.VMEM)
    hbm = pl.BlockSpec(memory_space=pltpu.HBM)
    dma = pltpu.SemaphoreType.DMA
    result = pl.pallas_call(
        kernel,
        out_shape=jax.ShapeDtypeStruct((16 * 6 * ROWS, LANES), f32),
        in_specs=[hbm] * 4,
        out_specs=vmem,
        scratch_shapes=[
            pltpu.VMEM((16 * 3 * ROWS, LANES), f32),
            pltpu.SMEM((16,), jnp.int32),
            pltpu.SMEM((NMAT, 8), f32),
            pltpu.VMEM((KA, 8 + 3 * PART * 16, LANES), f32),
            pltpu.VMEM((KA, 8 + 3 * PART * 16, LANES), f32),
            pltpu.VMEM((2, KA, PART, 6, 8, LANES), f32),
            pltpu.VMEM((512, 256), jnp.bfloat16),
            *[pltpu.VMEM((2, ALL_ROWS, 6, 8, LANES), f32)] * 6,
            pltpu.VMEM((2, 2, 8, 6, 8, LANES), f32),
            pltpu.VMEM((2, 2, 8, 6, 8, LANES), f32),
            pltpu.VMEM((2, 2, 6, 8, LANES), f32),
            pltpu.VMEM((2, 4, 6, 8, LANES), f32),
            pltpu.VMEM((8, 8, LANES), jnp.int32),
            pltpu.VMEM((2, 8, LANES), jnp.int32),
            pltpu.VMEM((2, 8, 8, LANES), f32),
            pltpu.VMEM((8, 64, LANES), f32),
            pltpu.VMEM((2, 64, 7, 8, LANES), f32),
            pltpu.VMEM((2, 5, 8, LANES), f32),
            dma((2, KA)),
            dma((2, KA)),
            dma((3, KA)),
            dma((3, KA)),
            dma((2, 8)),
            dma((2, 8)),
            dma((4,)),
            dma((4,)),
            dma((4,)),
        ],
        compiler_params=pltpu.CompilerParams(
            collective_id=0, has_side_effects=True, vmem_limit_bytes=48 * 2**20
        ),
        name="adjoint",
    )(loads.reshape(16 * 3 * ROWS, LANES), sleeper_pos, material.reshape(ROWS // 8, 8, LANES), material_table)
    return result.reshape(16, 2, 3, ROWS, LANES)


def solution(mesh):
    return jax.shard_map(
        local,
        mesh=mesh,
        in_specs=(P("ka", None, "gy", "gz"), P("ka"), P("gy", "gz"), P()),
        out_specs=P("ka", None, None, "gy", "gz"),
        check_vma=False,
    )
```

```python
import math

import jax
import jax.numpy as jnp
from jax import lax
from jax.experimental import pallas as pl
from jax.experimental.pallas import tpu as pltpu
from jax.sharding import PartitionSpec as P

KW = 128
NMAT = 8
KA, GY, GZ = 8, 8, 4
LANES = 128
ROWS = 32
PART = ROWS // KA
STEPS = 7
STRIP = 21
TOP, LEFT, RIGHT, ALL_ROWS = 8, 49, 59, 68
MESH = pl.DeviceIdType.MESH
f32 = jnp.float32


def sine(angle):
    square = angle * angle
    value = jnp.full_like(angle, 1.0 / math.factorial(13))
    for degree in (11, 9, 7, 5, 3, 1):
        sign = -1.0 if (degree // 2) % 2 else 1.0
        value = value * square + sign / math.factorial(degree)
    return value * angle


def kernel(
    loads_hbm, pos_hbm, material_hbm, table_hbm, out_hbm,
    out, loads, pos, table, s1, r1, s2, wm, f_b, f_a, f_c, f_u, f_r, f_o,
    strip_out, strip_in, corner_out, corner_in, mat, mat_in, mask, cells, coupling, per_k,
    p1_send, p1_recv, p2_send, p2_recv, halo_send, halo_recv, mat_send, mat_recv, in_sem, out_sem,
):
    ka, gy, gz = lax.axis_index("ka"), lax.axis_index("gy"), lax.axis_index("gz")
    shape = (8, LANES)
    sub = lax.broadcasted_iota(jnp.int32, shape, 0)
    lane = lax.broadcasted_iota(jnp.int32, shape, 1)

    barrier = pltpu.get_barrier_semaphore()
    for o in range(1, KA):
        pl.semaphore_signal(
            barrier, inc=1, device_id={"ka": (ka + o) % KA}, device_id_type=MESH
        )
    for dy in (-1, 0, 1):
        for dz in (-1, 0, 1):
            if dy or dz:
                pl.semaphore_signal(
                    barrier,
                    inc=1,
                    device_id={"gy": (gy + dy + GY) % GY, "gz": (gz + dz + GZ) % GZ},
                    device_id_type=MESH,
                )

    arguments = [
        pltpu.make_async_copy(src, dst, in_sem.at[n])
        for n, (src, dst) in enumerate(
            (
                (pos_hbm, pos),
                (loads_hbm, loads),
                (material_hbm, mat.at[pl.ds(1, ROWS // 8)]),
                (table_hbm, table),
            )
        )
    ]
    for copy in arguments:
        copy.start()
    arguments[0].wait()

    position = jnp.zeros(shape, jnp.int32)
    for s in range(16):
        position = jnp.where(lane == ka * 16 + s, pos[s], position)
    position = position.astype(f32)
    arguments[1].wait()

    def stage(o, carry):
        first = ((ka + o) % KA) * PART
        s1[o, 0:8, :] = position
        for h in range(2):
            for yy in range(PART):
                for comp in range(3):
                    start = h * 8 * 96 + comp * ROWS + first + yy
                    at = 8 + (yy * 3 + comp) * 16 + h * 8
                    s1[o, at : at + 8, :] = loads[pl.ds(start, 8, stride=96), :]
        return carry

    lax.fori_loop(0, KA, stage, 0)
    zero = jnp.zeros(shape, f32)

    def clear_rows(first):
        def body(row, carry):
            for buffer in (f_b, f_a, f_c, f_u, f_r):
                for g in range(2):
                    for c in range(6):
                        buffer[g, row, c] = zero
            return carry

        lax.fori_loop(first, first + 8, body, 0)

    pl.when(gy == 0)(lambda: clear_rows(0))
    pl.when(gy == GY - 1)(lambda: clear_rows(TOP + ROWS))
    arguments[2].wait()
    arguments[3].wait()

    pl.semaphore_wait(barrier, KA - 1 + 8)

    exists = {-1: gy > 0, 1: gy < GY - 1}, {-1: gz > 0, 1: gz < GZ - 1}

    def send(src, dst, dy, dz, sends, recvs, at):
        copy = pltpu.make_async_remote_copy(
            src_ref=src,
            dst_ref=dst,
            send_sem=sends.at[at],
            recv_sem=recvs.at[at],
            device_id={"gy": (gy + dy + GY) % GY, "gz": (gz + dz + GZ) % GZ},
            device_id_type=MESH,
        )
        to, origin = True, True
        if dy:
            to, origin = exists[0][dy], exists[0][-dy]
        if dz:
            to = exists[1][dz] if to is True else jnp.logical_and(to, exists[1][dz])
            origin = exists[1][-dz] if origin is True else jnp.logical_and(origin, exists[1][-dz])
        return copy, to, origin

    def start(message):
        pl.when(message[1])(lambda: message[0].start())

    def finish(message):
        pl.when(message[1])(lambda: message[0].wait_send())

    def receive(message):
        pl.when(message[2])(lambda: message[0].wait_recv())

    mat_rows = (
        send(mat.at[1], mat.at[5], -1, 0, mat_send, mat_recv, 0),
        send(mat.at[4], mat.at[0], 1, 0, mat_send, mat_recv, 1),
    )
    mat_strips = (
        send(mat.at[6], mat_in.at[0], 0, 1, mat_send, mat_recv, 2),
        send(mat.at[7], mat_in.at[1], 0, -1, mat_send, mat_recv, 3),
    )
    for message in mat_rows:
        start(message)

    early, late = pl.ds(0, 8 + PART * 24), pl.ds(8 + PART * 24, PART * 24)

    def copy1(part, o, source):
        rows = late if part else early
        return pltpu.make_async_remote_copy(
            src_ref=s1.at[o, rows],
            dst_ref=r1.at[source, rows],
            send_sem=p1_send.at[part, o],
            recv_sem=p1_recv.at[part, o],
            device_id={"ka": (ka + o) % KA},
            device_id_type=MESH,
        )

    far_first = (4, 3, 5, 2, 6, 1, 7)
    for o in far_first:
        copy1(0, o, ka).start()
    r1[ka] = s1[0]

    block = lane // STRIP
    place = lane - block * STRIP
    for message in mat_rows:
        receive(message)
    for side in range(2):
        value = mat[5]
        value = pltpu.roll(value, (STRIP * 5 + 7 + 7 * side) % LANES, 1)
        for j in range(5):
            value = jnp.where(block == j, pltpu.roll(mat[j], STRIP * j + 7 + 7 * side, 1), value)
        mat[6 + side] = value
    for message in mat_strips:
        start(message)

    for side in range(2):
        row = gy * ROWS + 8 * block - 8
        column = gz * LANES + place + (LANES - 14 if side else -7)
        inside = jnp.logical_and(column >= 0, column < GZ * LANES)
        inside = jnp.logical_and(inside, block < 6)
        for i in range(8):
            valid = jnp.logical_and(row + i >= 0, row + i < GY * ROWS)
            if i == 0:
                valid = jnp.logical_and(valid, block > 0)
            if i == 7:
                valid = jnp.logical_and(valid, block < 5)
            mask[side, i] = jnp.where(jnp.logical_and(inside, valid), 1.0, 0.0)

    squares, centers = [], []
    for g in range(2):
        k = ka * 16 + g * 8 + sub
        half_turn = jnp.minimum(k, KW - k).astype(f32) * (math.pi / KW)
        root = 2.0 * sine(half_turn)
        q = root * root
        low, high = None, None
        for m in range(NMAT):
            entry = [jnp.full(shape, table[m, f], f32) for f in range(7)]
            off = [jnp.abs(entry[f]) for f in (4, 5, 6)]
            sums = (off[0] + off[1], off[0] + off[2], off[1] + off[2])
            lo = [entry[1 + c] - sums[c] for c in range(3)]
            hi = [entry[1 + c] + sums[c] for c in range(3)]
            lo = entry[0] + jnp.minimum(jnp.minimum(lo[0], lo[1]), lo[2]) * q
            hi = entry[0] + jnp.maximum(jnp.maximum(hi[0], hi[1]), hi[2]) * q
            low = lo if low is None else jnp.minimum(low, lo)
            high = hi if high is None else jnp.maximum(high, hi)
        high = 8.0 + high
        center = 0.5 * (high + low)
        width = 0.5 * (high - low)
        ratio = center / width
        weight = 1.0 / ratio
        d = [1.0 / center]
        r = [jnp.ones(shape, f32)]
        u = list(d)
        for _ in range(3):
            r = r + [zero]
            lowered = [center * d[j] if j < len(d) else zero for j in range(len(r))]
            raised = [zero] + d
            r = [r[j] - lowered[j] + raised[j] for j in range(len(r))]
            new_weight = 1.0 / (2.0 * ratio - weight)
            d = [
                (new_weight * weight) * (d[j] if j < len(d) else zero)
                + (2.0 * new_weight / width) * r[j]
                for j in range(len(r))
            ]
            u = [(u[j] if j < len(u) else zero) + d[j] for j in range(len(d))]
            weight = new_weight
        for j in range(4):
            per_k[g, j] = u[j]
        per_k[g, 4] = center
        squares.append(q)
        centers.append(center)

    for o in far_first:
        copy1(0, o, ka).wait_send()
        copy1(1, o, ka).start()

    for message in mat_strips:
        receive(message)
    foreign = (place < 7, place >= 14)
    mat_strip = [jnp.where(foreign[side], mat_in[side], mat[6 + side]) for side in range(2)]

    def gather_cells(t, carry):
        index = mat[t]
        rows = pl.ds(pl.multiple_of(t * 8, 8), 8)
        for f in range(8):
            value = jnp.zeros(shape, f32)
            for m in range(NMAT):
                value = jnp.where(index == m, table[m, f], value)
            cells[f, rows, :] = value
        return carry

    lax.fori_loop(0, 6, gather_cells, 0)
    for side in range(2):
        for f in range(8):
            value = jnp.zeros(shape, f32)
            for m in range(NMAT):
                value = jnp.where(mat_strip[side] == m, table[m, f], value)
            cells[f, 48 + 8 * side : 56 + 8 * side, :] = value

    def prepare_coupling(y, carry):
        row = [cells[f, pl.ds(y, 1), :] for f in range(8)]
        for g in range(2):
            q = squares[g]
            base = centers[g] - 4.0 - row[0]
            for c in range(3):
                coupling[g, y, c] = base - q * row[1 + c]
                coupling[g, y, 3 + c] = -(q * row[4 + c])
            coupling[g, y, 6] = q * row[7]
        return carry

    lax.fori_loop(0, 64, prepare_coupling, 0)

    for o in range(1, KA):
        copy1(0, o, (ka + KA - o) % KA).wait_recv()
    positions = r1[0, 0:1, :]
    for i in range(1, KA):
        positions += r1[i, 0:1, :]
    positions = jnp.broadcast_to(positions, (256, LANES)).astype(jnp.int32)
    wide = (256, LANES)
    row_no = lax.broadcasted_iota(jnp.int32, wide, 0)
    k_of = (row_no // 16) * 8 + row_no % 8
    imaginary = (row_no // 8) % 2
    turn = (k_of * positions + 32 * imaginary) & (KW - 1)
    away = jnp.abs(turn - KW // 2) - KW // 4
    weights = sine(away.astype(f32) * (2.0 * math.pi / KW))
    w_hi = weights.astype(jnp.bfloat16)
    w_lo = (weights - w_hi.astype(f32)).astype(jnp.bfloat16)
    wm[0:256, 0:128] = w_hi
    wm[0:256, 128:256] = w_hi
    wm[256:512, 0:128] = w_lo
    wm[256:512, 128:256] = jnp.zeros((256, 128), jnp.bfloat16)

    def transform(yy, carry):
        for comp in range(3):
            row = pl.ds(pl.multiple_of(8 + (yy * 3 + comp) * 16, 8), 16)
            values = jnp.concatenate([r1[i, row, :] for i in range(KA)], axis=0)
            v_hi = values.astype(jnp.bfloat16)
            v_lo = (values - v_hi.astype(f32)).astype(jnp.bfloat16)
            product = jnp.dot(
                wm[...], jnp.concatenate([v_hi, v_lo], axis=0), preferred_element_type=f32
            )
            product = product[0:256] + product[256:512]
            for d in range(KA):
                for g in range(2):
                    for ri in range(2):
                        at = ((d * 2 + g) * 2 + ri) * 8
                        s2[g, d, yy, ri * 3 + comp] = product[at : at + 8]
        return carry

    first_row = (0, PART // 2, 0)
    row_count = (PART // 2, PART // 2, PART)

    def copy2(part, o, source):
        g, first, count = part // 2, first_row[part], row_count[part]
        return pltpu.make_async_remote_copy(
            src_ref=s2.at[g, (ka + o) % KA, pl.ds(first, count)],
            dst_ref=f_b.at[g, pl.ds(TOP + PART * source + first, count)],
            send_sem=p2_send.at[part, o],
            recv_sem=p2_recv.at[part, o],
            device_id={"ka": (ka + o) % KA},
            device_id_type=MESH,
        )

    lax.fori_loop(0, PART // 2, transform, 0)
    for o in far_first:
        copy2(0, o, ka).start()
    for o in range(1, KA):
        copy1(1, o, (ka + KA - o) % KA).wait_recv()
    lax.fori_loop(PART // 2, PART, transform, 0)
    for o in far_first:
        copy2(1, o, ka).start()
    for g in range(2):
        f_b[g, pl.ds(TOP + PART * ka, PART)] = s2[g, ka]
    for o in far_first:
        copy2(0, o, ka).wait_send()
    for o in far_first:
        copy2(1, o, ka).wait_send()
        copy2(2, o, ka).start()

    def messages(g):
        rows = (
            send(f_b.at[g, pl.ds(TOP, 7)], f_b.at[g, pl.ds(TOP + ROWS, 7)], -1, 0, halo_send, halo_recv, (g, 0)),
            send(f_b.at[g, pl.ds(TOP + ROWS - 7, 7)], f_b.at[g, pl.ds(1, 7)], 1, 0, halo_send, halo_recv, (g, 1)),
        )
        sides = (
            send(strip_out.at[g, 0], strip_in.at[g, 0], 0, 1, halo_send, halo_recv, (g, 2)),
            send(strip_out.at[g, 1], strip_in.at[g, 1], 0, -1, halo_send, halo_recv, (g, 3)),
        )
        corners = tuple(
            send(corner_out.at[g, n // 2], corner_in.at[g, n], dy, dz, halo_send, halo_recv, (g, 4 + n))
            for n, (dy, dz) in enumerate(((1, 1), (1, -1), (-1, 1), (-1, -1)))
        )
        return rows, sides + corners

    def exchange(g):
        for part in (2,) if g else (0, 1):
            for o in far_first:
                copy2(part, o, (ka + KA - o) % KA).wait_recv()
        rows, others = messages(g)
        for message in rows:
            start(message)

        def body(c, carry):
            near = [zero, zero]
            for i in range(8):
                values = [f_b[g, TOP + 8 * j + i, c] for j in range(4)]
                for side in range(2):
                    shift = 7 + 7 * side
                    strip = pltpu.roll(values[3], (STRIP * 4 + shift) % LANES, 1)
                    for j in (2, 1, 0):
                        strip = jnp.where(
                            block <= j + 1, pltpu.roll(values[j], STRIP * (j + 1) + shift, 1), strip
                        )
                    strip_out[g, side, i, c] = strip
                here = jnp.logical_and(lane >= 14 * i, lane < 14 * i + 14)
                near[0] = jnp.where(here, pltpu.roll(values[3], 14 * i + 7, 1), near[0])
                near[1] = jnp.where(here, pltpu.roll(values[0], 14 * i + 7, 1), near[1])
            corner_out[g, 0, c] = near[0]
            corner_out[g, 1, c] = near[1]
            return carry

        lax.fori_loop(0, 6, body, 0, unroll=2)
        for message in others:
            start(message)

    inner_block = jnp.logical_and(block >= 1, block <= 4)

    def wrap_strips(buffer, g, c):
        for first in (LEFT, RIGHT):
            buffer[g, first - 1, c] = pltpu.roll(buffer[g, first + 7, c], STRIP, 1)
            buffer[g, first + 8, c] = pltpu.roll(buffer[g, first, c], LANES - STRIP, 1)

    def assemble(g):
        masks = [[mask[side, i] > 0.5 for i in range(8)] for side in range(2)]

        def body(c, carry):
            for i in range(8):
                above, below = f_b[g, i, c], f_b[g, TOP + ROWS + i, c]
                for side in range(2):
                    shift = 7 + 7 * side
                    own = jnp.where(
                        block == 0,
                        pltpu.roll(above, shift, 1),
                        jnp.where(
                            block == 5,
                            pltpu.roll(below, (STRIP * 5 + shift) % LANES, 1),
                            strip_out[g, side, i, c],
                        ),
                    )
                    lower = 2 * LANES + 7 * side - 14 * i
                    other = jnp.where(
                        block == 0,
                        pltpu.roll(corner_in[g, side, c], lower % LANES, 1),
                        jnp.where(
                            block == 5,
                            pltpu.roll(corner_in[g, 2 + side, c], (lower + STRIP * 5) % LANES, 1),
                            strip_in[g, side, i, c],
                        ),
                    )
                    value = jnp.where(foreign[side], other, own)
                    f_b[g, (LEFT, RIGHT)[side] + i, c] = jnp.where(masks[side][i], value, 0.0)
            return carry

        lax.fori_loop(0, 6, body, 0, unroll=2)
        for c in range(6):
            wrap_strips(f_b, g, c)

    source = (f_b, f_a, f_c, f_u, f_r, f_a, f_c)
    target = (f_a, f_c, f_u, f_r, f_a, f_c, f_o)

    def advance(e, g, at, cell, keep=None):
        src = source[e]
        here = [src[g, at, c] for c in range(6)]
        k = [coupling[g, cell, f] for f in range(7)]
        scale = per_k[g, (2, 1, 0, 4, 2, 1, 0)[e]]
        for c in range(6):
            comp, other = c % 3, (c + 3) % 6
            value = src[g, at - 1, c] + src[g, at + 1, c]
            value += pltpu.roll(here[c], 1, 1) + pltpu.roll(here[c], LANES - 1, 1)
            value += k[comp] * here[c]
            for j in range(3):
                if j != comp:
                    value += k[2 + comp + j] * here[c - comp + j]
            if c < 3:
                value += k[6] * here[other]
            else:
                value -= k[6] * here[other]
            if e in (0, 4):
                value = per_k[g, 3] * value + scale * here[c]
            elif e in (1, 2):
                value += scale * f_b[g, at, c]
            elif e == 3:
                value = f_b[g, at, c] + (value - scale * here[c])
            else:
                value += scale * f_r[g, at, c]
            if e == 6:
                value += f_u[g, at, c]
            if keep is not None:
                value *= keep
            target[e][g, at, c] = value

    def main_rows(e, g, first, count, unroll):
        def body(i, carry):
            advance(e, g, i + first, i + first)
            return carry

        lax.fori_loop(0, count, body, 0, unroll=unroll)

    def interior(g):
        for e in range(STEPS):
            main_rows(e, g, TOP + e + 1, 30 - 2 * e, (15, 14, 13, 12, 11, 10, 9)[e])

    def borders_and_strips(g):
        above = jnp.where(gy > 0, 1.0, 0.0)
        below = jnp.where(gy < GY - 1, 1.0, 0.0)
        for e in range(STEPS):

            def body(i, carry):
                at = TOP - 6 + e + i
                advance(e, g, at, at, jnp.where(i < 6 - e, above, 1.0))
                at = TOP + ROWS - 2 - e + i
                advance(e, g, at, at, jnp.where(i >= e + 2, below, 1.0))
                advance(e, g, LEFT + i, 48 + i, mask[0, i])
                advance(e, g, RIGHT + i, 56 + i, mask[1, i])
                return carry

            lax.fori_loop(0, 8, body, 0, unroll=8)
            if e < STEPS - 1:
                for c in range(6):
                    wrap_strips(target[e], g, c)

    def deliver(g):
        edge = jnp.logical_or(lane < 7, lane >= LANES - 7)

        def body(i, carry):
            for c in range(6):
                joined = jnp.where(
                    place < 7, pltpu.roll(f_o[g, RIGHT + i, c], LANES - 7, 1), f_o[g, LEFT + i, c]
                )
                for j in range(4):
                    y = 8 * j + i
                    value = jnp.where(
                        edge,
                        pltpu.roll(joined, (2 * LANES - STRIP * (j + 1) - 7) % LANES, 1),
                        f_o[g, TOP + y, c],
                    )
                    out[pl.ds(g * 8 * 192 + c * ROWS + y, 8, stride=192), :] = value
            return carry

        lax.fori_loop(0, 8, body, 0, unroll=4)

    def result(g):
        rows = pl.ds(g * 8 * 192, 8 * 192)
        return pltpu.make_async_copy(out.at[rows], out_hbm.at[rows], out_sem.at[g])

    def await_halo(g):
        for group in messages(g):
            for message in group:
                receive(message)

    exchange(0)
    interior(0)
    await_halo(0)
    assemble(0)
    exchange(1)
    borders_and_strips(0)
    deliver(0)
    result(0).start()
    interior(1)
    await_halo(1)
    assemble(1)
    borders_and_strips(1)
    deliver(1)
    result(1).start()

    for o in range(1, KA):
        copy1(1, o, ka).wait_send()
        copy2(2, o, ka).wait_send()
    result(0).wait()
    result(1).wait()
    for message in mat_rows + mat_strips:
        finish(message)
    for g in range(2):
        for group in messages(g):
            for message in group:
                finish(message)


def local(loads, sleeper_pos, material, material_table):
    hbm = pl.BlockSpec(memory_space=pltpu.HBM)
    dma = pltpu.SemaphoreType.DMA
    result = pl.pallas_call(
        kernel,
        out_shape=jax.ShapeDtypeStruct((16 * 6 * ROWS, LANES), f32),
        in_specs=[hbm] * 4,
        out_specs=hbm,
        scratch_shapes=[
            pltpu.VMEM((16 * 6 * ROWS, LANES), f32),
            pltpu.VMEM((16 * 3 * ROWS, LANES), f32),
            pltpu.SMEM((16,), jnp.int32),
            pltpu.SMEM((NMAT, 8), f32),
            pltpu.VMEM((KA, 8 + 3 * PART * 16, LANES), f32),
            pltpu.VMEM((KA, 8 + 3 * PART * 16, LANES), f32),
            pltpu.VMEM((2, KA, PART, 6, 8, LANES), f32),
            pltpu.VMEM((512, 256), jnp.bfloat16),
            *[pltpu.VMEM((2, ALL_ROWS, 6, 8, LANES), f32)] * 6,
            pltpu.VMEM((2, 2, 8, 6, 8, LANES), f32),
            pltpu.VMEM((2, 2, 8, 6, 8, LANES), f32),
            pltpu.VMEM((2, 2, 6, 8, LANES), f32),
            pltpu.VMEM((2, 4, 6, 8, LANES), f32),
            pltpu.VMEM((8, 8, LANES), jnp.int32),
            pltpu.VMEM((2, 8, LANES), jnp.int32),
            pltpu.VMEM((2, 8, 8, LANES), f32),
            pltpu.VMEM((8, 64, LANES), f32),
            pltpu.VMEM((2, 64, 7, 8, LANES), f32),
            pltpu.VMEM((2, 5, 8, LANES), f32),
            dma((2, KA)),
            dma((2, KA)),
            dma((3, KA)),
            dma((3, KA)),
            dma((2, 8)),
            dma((2, 8)),
            dma((4,)),
            dma((4,)),
            dma((4,)),
            dma((2,)),
        ],
        compiler_params=pltpu.CompilerParams(
            collective_id=0, has_side_effects=True, vmem_limit_bytes=60 * 2**20
        ),
        name="adjoint",
    )(loads.reshape(16 * 3 * ROWS, LANES), sleeper_pos, material.reshape(ROWS // 8, 8, LANES), material_table)
    return result.reshape(16, 2, 3, ROWS, LANES)


def solution(mesh):
    return jax.shard_map(
        local,
        mesh=mesh,
        in_specs=(P("ka", None, "gy", "gz"), P("ka"), P("gy", "gz"), P()),
        out_specs=P("ka", None, None, "gy", "gz"),
        check_vma=False,
    )
```
